32 devices in a mesh: az: 8 (over y, x, core), rad: 4 (over z).
Axes of the slice: x: 2, y: 2, z: 4, core: 2. Of those that a mesh axis runs over, the one named last changes fastest.
Arguments:
- fields: float32 [2, 128, 8, 4096], P(None, 'rad', None, 'az'), may hold values from 0.1 to 2
- cycle_blocks: int32 [128, 1], P('rad'), may hold values from 0 to 7, as said below
- cycle_cells: int32 [128], P('rad'), may hold values from 0 to 511
- cycle_fracs: float32 [128], P('rad'), may hold values from 0 to 1
- coupling: float32 [2, 128], P(None, 'rad'), may hold values from 300 to 3000
Outputs:
- evolved: float32 [2, 128, 8, 4096], P(None, 'rad', None, 'az')
The draws below stay inside these ranges and needn't reach their ends.
Inputs may be any that keep to these rules, and one draw needn't show every extreme that they name: `cycle_blocks`: in each aligned block of 32 cycles (the cycles of one index of rad) no value is named by more than 8 cycles.
All inputs are finite; a program needn't handle non-finite values.
Results may differ from the reference program's by a relative error of at most 0.0003.
Values sent between devices are 32-bit elements; how exact they have to be, the bound alone decides.
No kernel may reach another device: no remote copies, remote signals or barrier semaphores. Data moves between devices by JAX's collectives and lax.ppermute only.
A program may use at most 128 MiB of HBM per device.

```python
import math
import jax
import jax.numpy as jnp
from jax import lax

FL = 2
NZ = 8
RD = 32
AD = 512
NR = 128
NA = 4096
MOST = 8
N_AZ = 8
N_RAD = 4


def shear_profile(key):
    inner_key = jax.random.fold_in(key, 31)
    base = jax.random.randint(jax.random.fold_in(inner_key, 1), (), 0, N_AZ).astype(jnp.int32)
    group_ids = jnp.arange(N_RAD, dtype=jnp.int32)
    steps_out = N_RAD - 1 - group_ids
    run_of_group = jnp.maximum(1, MOST // (1 + steps_out * 3 // N_RAD)).astype(jnp.int32)
    runs_in_group = (RD + run_of_group - 1) // run_of_group
    runs_before = (jnp.cumsum(runs_in_group) - runs_in_group).astype(jnp.int32)
    cycle = jnp.arange(NR, dtype=jnp.int32)
    group = cycle // RD
    local = cycle % RD
    run_len = run_of_group[group]
    run_index = runs_before[group] + local // run_len
    blocks = ((base - run_index) % N_AZ).astype(jnp.int32)
    span = jnp.maximum(1, AD // run_len)
    noise = jax.random.randint(jax.random.fold_in(inner_key, 2), (NR,), 0, 1 << 20).astype(jnp.int32)
    jitter = noise % span
    cells = AD - 1 - local % run_len * AD // run_len - jitter
    cells = jnp.where(local == 0, AD - 1, cells)
    cells = jnp.where(local == RD - 1, 0, cells)
    return (blocks, jnp.clip(cells, 0, AD - 1).astype(jnp.int32))


def draw_cycle_blocks(key, part):
    blocks, cells = shear_profile(key)
    return blocks[:, None]


def draw_cycle_cells(key, part):
    blocks, cells = shear_profile(key)
    return cells


def block_levels(stream_key, extent, split, low, largest):
    gain, own = 1.0, jax.random.fold_in(stream_key, 6)
    for dim, shards_of in split:
        steps = jnp.exp(jax.random.uniform(jax.random.fold_in(own, dim), (shards_of,), jnp.float32, low / len(split), largest / len(split)))
        gain = gain * jnp.repeat(steps, extent[dim] // shards_of).reshape([-1 if axis == dim else 1 for axis in range(len(extent))])
    return gain


def setup_inputs(seed: int = 0) -> dict:
    arg_keys = jax.random.split(jax.random.key(seed), 6)
    fields = jnp.clip(jnp.exp(math.log(2.0) - 2.9957323 * jax.random.uniform(arg_keys[0], (FL, NR, NZ, NA), jnp.float32) ** block_levels(arg_keys[0], (FL, NR, NZ, NA), ((1, 4), (3, 8)), -0.2, 0.2)), 0.1, 2.0)
    cycle_blocks = draw_cycle_blocks(jax.random.fold_in(arg_keys[5], 71), 0)
    cycle_cells = draw_cycle_cells(jax.random.fold_in(arg_keys[5], 71), 0)
    cycle_fracs = jnp.clip(1.0 * jax.random.uniform(arg_keys[3], (NR,), jnp.float32) ** block_levels(arg_keys[3], (NR,), ((0, 4),), -0.2, 0.2), 0.0, 1.0)
    coupling = jnp.clip(jnp.exp(math.log(3000.0) - 2.3025851 * jax.random.uniform(arg_keys[4], (FL, NR), jnp.float32) ** block_levels(arg_keys[4], (FL, NR), ((1, 4),), -0.2, 0.2)), 300.0, 3000.0)
    return {"fields": fields, "cycle_blocks": cycle_blocks, "cycle_cells": cycle_cells, "cycle_fracs": cycle_fracs, "coupling": coupling}


def cycle_take(cycle, places):
    return jnp.take(cycle, places, axis=-1)

def reference(fields, cycle_blocks, cycle_cells, cycle_fracs, coupling):
    offset = AD * cycle_blocks[:, 0] + cycle_cells
    column = jnp.arange(NA, dtype=jnp.int32)
    near_place = ((column[None, :] - offset[:, None]) % NA).astype(jnp.int32)
    far_place = ((column[None, :] - offset[:, None] - 1) % NA).astype(jnp.int32)
    nearer = jax.vmap(cycle_take, in_axes=(1, 0), out_axes=1)(fields, near_place)
    farther = jax.vmap(cycle_take, in_axes=(1, 0), out_axes=1)(fields, far_place)
    weight = cycle_fracs[None, :, None, None]
    shifted = (1.0 - weight) * nearer + weight * farther
    zero_col = jnp.zeros((FL, 1), coupling.dtype)
    coupled = jnp.concatenate([zero_col, coupling[:, 1:]], axis=1)
    outer = jnp.concatenate([coupled[:, 1:], zero_col], axis=1)
    lower_band = -coupled
    main_band = 1.0 + coupled + outer
    upper_band = -outer
    right_side = shifted.reshape(FL, NR, NZ * NA)
    solved = lax.linalg.tridiagonal_solve(lower_band, main_band, upper_band, right_side)
    return solved.reshape(shifted.shape)
```

```python
import functools

import jax
import jax.numpy as jnp
from jax import lax
from jax.experimental import pallas as pl
from jax.experimental.pallas import tpu as pltpu
from jax.sharding import PartitionSpec as P

LANES = 128
SUBLANES = 8
VMEM_LIMIT = 24 * 1024 * 1024


def smem():
    return pl.BlockSpec(memory_space=pltpu.SMEM)


def params():
    return pltpu.CompilerParams(vmem_limit_bytes=VMEM_LIMIT)


def cost(flops, moved):
    return pl.CostEstimate(flops=flops, bytes_accessed=moved, transcendentals=0)


def sent_along(block, axis, distance):
    size = lax.axis_size(axis)
    return lax.ppermute(block, axis, [(i, (i + distance) % size) for i in range(size)])


def partner_of(rank, step, size):
    if size & (size - 1) == 0:
        return rank ^ step, rank ^ step
    return (rank + step) % size, (rank - step) % size


def exchanged(block, axis, step):
    size = lax.axis_size(axis)
    return lax.ppermute(block, axis, [(i, partner_of(i, step, size)[0]) for i in range(size)])


def spread_kernel(vertical, x_ref, *refs):
    out_refs, (held, sems) = refs[:-2], refs[-2:]
    chunks, rows = held.shape[0], held.shape[1] // vertical
    copies = [
        pltpu.make_async_copy(x_ref.at[:, q * LANES : (q + 1) * LANES], held.at[q], sems.at[q])
        for q in range(chunks)
    ]
    for copy in copies:
        copy.start()
    lane = lax.broadcasted_iota(jnp.int32, (SUBLANES, LANES), 1)
    for q in range(chunks):
        copies[q].wait()
        for z in range(vertical):
            out_refs[z][q * rows : (q + 1) * rows, :] = held[q, pl.ds(z, rows, stride=vertical), :]
    out_refs[0][chunks * rows :, :] = jnp.zeros((SUBLANES, LANES), jnp.float32)
    for z in range(vertical):
        tile = jnp.zeros((SUBLANES, LANES), jnp.float32)
        for g in range(rows // SUBLANES):
            start = (chunks - 1) * rows + g * SUBLANES
            last = out_refs[z][start : start + SUBLANES, :]
            tile = jnp.where(lane == g, pltpu.roll(last, g + 1, 1), tile)
        if z + 1 < vertical:
            out_refs[z + 1][chunks * rows :, :] = tile
        else:
            out_refs[vertical][...] = tile


def spread(x, vertical):
    total, width = x.shape
    rows = total // vertical
    main = jax.ShapeDtypeStruct((rows * width // LANES + SUBLANES, LANES), jnp.float32)
    tail = jax.ShapeDtypeStruct((SUBLANES, LANES), jnp.float32)
    chunks = width // LANES
    return pl.pallas_call(
        functools.partial(spread_kernel, vertical),
        out_shape=[main] * vertical + [tail],
        in_specs=[pl.BlockSpec(memory_space=pl.ANY)],
        scratch_shapes=[
            pltpu.VMEM((chunks, total, LANES), jnp.float32),
            pltpu.SemaphoreType.DMA((chunks,)),
        ],
        compiler_params=params(),
        cost_estimate=cost(0, 2 * total * width * 4),
    )(x)


def turn_kernel(vertical, devices, fluids, blocks, cells, fracs, *refs):
    in_refs = refs[:vertical]
    tail_ref = refs[vertical]
    out_refs = refs[vertical + 1 : vertical + 1 + devices]
    held, edge, sorted_ref = refs[vertical + 1 + devices :]
    chunks, rows = held.shape[0], held.shape[1] // vertical
    width = chunks * LANES
    cycles = rows // fluids
    for z in range(vertical):
        for q in range(chunks):
            held[q, pl.ds(z, rows, stride=vertical), :] = in_refs[z][q * rows : (q + 1) * rows, :]
        if z + 1 < vertical:
            tile = in_refs[z + 1][chunks * rows :, :]
        else:
            tile = tail_ref[...]
        for g in range(rows // SUBLANES):
            turned = tile if g == 0 else pltpu.roll(tile, LANES - g, 1)
            edge[pl.ds(z + g * SUBLANES * vertical, SUBLANES, stride=vertical), :] = turned
    lane = lax.broadcasted_iota(jnp.int32, (vertical, width), 1)
    wide_lane = lax.broadcasted_iota(jnp.int32, (devices, width), 1)

    def one_cycle(r, carry):
        shift = cells[r]
        block = blocks[r, 0]
        weight = fracs[r]
        for f in range(fluids):
            row = f * cycles + r
            at = pl.ds(pl.multiple_of(row * vertical, vertical), vertical)
            near = jnp.concatenate([held[q, at, :] for q in range(chunks)], axis=1)
            far = jnp.where(lane == 0, edge[at, 0:1], pltpu.roll(near, 1, 1))
            mixed = (1.0 - weight) * near + weight * far
            mixed = pltpu.roll(mixed, shift, 1)
            if devices > vertical:
                pad = jnp.zeros((devices - vertical, width), jnp.float32)
                mixed = jnp.concatenate([mixed, pad], axis=0)
            first = pltpu.roll(mixed, lax.rem(devices - block, devices), 0)
            second = pltpu.roll(first, devices - 1, 0)
            to = pl.ds(pl.multiple_of(row * devices, devices), devices)
            chosen = jnp.where(wide_lane >= shift, first, second)
            for q in range(chunks):
                sorted_ref[q, to, :] = chosen[:, q * LANES : (q + 1) * LANES]
        return carry

    lax.fori_loop(0, cycles, one_cycle, 0)
    for e in range(devices):
        for q in range(chunks):
            out_refs[e][:, q * LANES : (q + 1) * LANES] = sorted_ref[
                q, pl.ds(e, rows, stride=devices), :
            ]


def turn(slices, tail, blocks, cells, fracs, fluids, width, devices):
    vertical = len(slices)
    cycles = cells.shape[0]
    rows = fluids * cycles
    out = jax.ShapeDtypeStruct((rows, width), jnp.float32)
    return pl.pallas_call(
        functools.partial(turn_kernel, vertical, devices, fluids),
        out_shape=[out] * devices,
        in_specs=[smem()] * 3 + [pl.BlockSpec()] * (vertical + 1),
        scratch_shapes=[
            pltpu.VMEM((width // LANES, rows * vertical, LANES), jnp.float32),
            pltpu.VMEM((rows * vertical, LANES), jnp.float32),
            pltpu.VMEM((width // LANES, rows * devices, LANES), jnp.float32),
        ],
        compiler_params=params(),
        cost_estimate=cost(0, 2 * rows * vertical * width * 4),
    )(blocks, cells, fracs, *slices, tail)


def coefficient_kernel(groups, own_ref, rank_ref, *refs):
    other_refs = refs[: groups - 1]
    coef_ref, link_ref = refs[groups - 1 : groups + 1]
    table, inner, outer, ahead, behind = refs[groups + 1 :]
    fluids, cycles = own_ref.shape
    total = groups * cycles
    rank = rank_ref[0]

    for step in range(groups):
        source = rank if step == 0 else rank_ref[step]
        ref = own_ref if step == 0 else other_refs[step - 1]

        def fill(r, carry, ref=ref, source=source):
            for f in range(fluids):
                table[f, source * cycles + r] = ref[f, r]
            return carry

        lax.fori_loop(0, cycles, fill, 0)
    for f in range(fluids):
        table[f, 0] = 0.0
        table[f, total] = 0.0

    def spans(f):
        return slice(f * LANES, (f + 1) * LANES)

    one = jnp.ones((1, LANES), jnp.float32)

    def pivots(s, carry):
        new = []
        for f in range(fluids):
            for way in range(2):
                here = carry[2 * f + way]
                link = jnp.full((1, LANES), table[f, s if way == 0 else total - s], jnp.float32)
                here = 1.0 + link * here / (link + here)
                if way == 0:
                    inner[s, :, spans(f)] = here
                else:
                    outer[total - 1 - s, :, spans(f)] = here
                new.append(here)
        return tuple(new)

    lax.fori_loop(0, total, pivots, (one,) * (2 * fluids))

    def ratios(r, carry):
        for f in range(fluids):
            link = jnp.full((1, LANES), table[f, r], jnp.float32)
            after = jnp.full((1, LANES), table[f, r + 1], jnp.float32)
            ahead[r, :, spans(f)] = after / (after + inner[r, :, spans(f)])
            behind[r, :, spans(f)] = link / (link + outer[r, :, spans(f)])
        return carry

    lax.fori_loop(0, total, ratios, 0)

    first = rank * cycles

    def upward(r, carry):
        new = []
        for f in range(fluids):
            at = (first + r, slice(None), spans(f))
            gain = 1.0 / (inner[at] + (outer[at] - 1.0))
            coef_ref[0, r, :, spans(f)] = ahead[at]
            coef_ref[1, r, :, spans(f)] = behind[at]
            coef_ref[2, r, :, spans(f)] = gain
            coef_ref[3, r, :, spans(f)] = gain * carry[2 * f]
            through = behind[at] * carry[2 * f + 1]
            coef_ref[6, r, :, spans(f)] = through
            new += [carry[2 * f] * ahead[at], through]
        return tuple(new)

    lax.fori_loop(0, cycles, upward, (one,) * (2 * fluids))

    def downward(s, carry):
        r = cycles - 1 - s
        new = []
        for f in range(fluids):
            at = (first + r, slice(None), spans(f))
            coef_ref[4, r, :, spans(f)] = coef_ref[2, r, :, spans(f)] * carry[2 * f]
            through = ahead[at] * carry[2 * f + 1]
            coef_ref[5, r, :, spans(f)] = through
            new += [carry[2 * f] * behind[at], through]
        return tuple(new)

    lax.fori_loop(0, cycles, downward, (one,) * (2 * fluids))

    for step in range(1, groups):
        source = rank_ref[step]
        inward = source < rank
        low = jnp.where(inward, source + 1, rank + 1) * cycles
        high = jnp.where(inward, rank, source) * cycles

        def through_blocks(r, carry, inward=inward):
            new = []
            for f in range(fluids):
                at = (r, slice(None), spans(f))
                new.append(carry[f] * jnp.where(inward, ahead[at], behind[at]))
            return tuple(new)

        product = lax.fori_loop(low, high, through_blocks, (one,) * fluids)
        none = jnp.zeros((1, LANES), jnp.float32)
        for f in range(fluids):
            link_ref[2 * (step - 1), :, spans(f)] = jnp.broadcast_to(
                jnp.where(inward, product[f], none), (SUBLANES, LANES)
            )
            link_ref[2 * (step - 1) + 1, :, spans(f)] = jnp.broadcast_to(
                jnp.where(inward, none, product[f]), (SUBLANES, LANES)
            )


def coefficients(own, ranks, others):
    fluids, cycles = own.shape
    groups = len(others) + 1
    total = groups * cycles
    wide = fluids * LANES
    per_cycle = pltpu.VMEM((total, 1, wide), jnp.float32)
    return pl.pallas_call(
        functools.partial(coefficient_kernel, groups),
        out_shape=[
            jax.ShapeDtypeStruct((7, cycles, 1, wide), jnp.float32),
            jax.ShapeDtypeStruct((2 * max(groups - 1, 1), SUBLANES, wide), jnp.float32),
        ],
        in_specs=[smem()] * (groups + 1),
        scratch_shapes=[pltpu.SMEM((fluids, total + 1), jnp.float32)] + [per_cycle] * 4,
        compiler_params=params(),
        cost_estimate=cost(0, 1 << 20),
    )(own, ranks, *others)


def coef_row(coef_ref, kind, r, f, chunks):
    row = coef_ref[kind, r, :, f * LANES : (f + 1) * LANES]
    return jnp.tile(row, (1, chunks))


def gather_kernel(vertical, devices, fluids, groups, blocks, cells, ranks, coef_ref, *refs):
    in_refs = refs[:devices]
    whole_ref = refs[devices]
    send_refs = refs[devices + 1 : devices + groups]
    (arrived,) = refs[devices + groups :]
    chunks, rows = arrived.shape[0], arrived.shape[1] // devices
    width = chunks * LANES
    cycles = rows // fluids
    for e in range(devices):
        for q in range(chunks):
            arrived[q, pl.ds(e, rows, stride=devices), :] = in_refs[e][
                :, q * LANES : (q + 1) * LANES
            ]
    lane = lax.broadcasted_iota(jnp.int32, (vertical, width), 1)

    def one_cycle(r, carry):
        shift = cells[r]
        block = blocks[r, 0]
        new = []
        for f in range(fluids):
            row = f * cycles + r
            at = pl.ds(pl.multiple_of(row * devices, devices), devices)
            held = jnp.concatenate([arrived[q, at, :] for q in range(chunks)], axis=1)
            first = pltpu.roll(held, block, 0)
            second = pltpu.roll(first, 1, 0)
            value = jnp.where(lane >= shift, first[:vertical], second[:vertical])
            whole_ref[pl.ds(pl.multiple_of(row * vertical, vertical), vertical), :] = value
            new.append(carry[2 * f] + coef_row(coef_ref, 5, r, f, chunks) * value)
            new.append(carry[2 * f + 1] + coef_row(coef_ref, 6, r, f, chunks) * value)
        return tuple(new)

    nothing = jnp.zeros((vertical, width), jnp.float32)
    sums = lax.fori_loop(0, cycles, one_cycle, (nothing,) * (2 * fluids))
    for step in range(1, groups):
        outward = ranks[groups - 1 + step] > ranks[0]
        for f in range(fluids):
            send_refs[step - 1][f] = jnp.where(outward, sums[2 * f], sums[2 * f + 1])


def gather(pieces, blocks, cells, ranks, coef, fluids, vertical, groups):
    devices = len(pieces)
    rows, width = pieces[0].shape
    edge = jax.ShapeDtypeStruct((fluids, vertical, width), jnp.float32)
    return pl.pallas_call(
        functools.partial(gather_kernel, vertical, devices, fluids, groups),
        out_shape=[jax.ShapeDtypeStruct((rows * vertical, width), jnp.float32)]
        + [edge] * (groups - 1),
        in_specs=[smem()] * 3 + [pl.BlockSpec()] * (devices + 1),
        scratch_shapes=[pltpu.VMEM((width // LANES, rows * devices, LANES), jnp.float32)],
        compiler_params=params(),
        cost_estimate=cost(0, 2 * rows * vertical * width * 4),
    )(blocks, cells, ranks, coef, *pieces)


def scan_kernel(vertical, fluids, coef_ref, whole_ref, out_ref):
    width = whole_ref.shape[1]
    cycles = whole_ref.shape[0] // vertical // fluids
    chunks = width // LANES

    def at(f, r):
        return pl.ds(pl.multiple_of((f * cycles + r) * vertical, vertical), vertical)

    def upward(r, carry):
        new = []
        for f in range(fluids):
            value = carry[f] + whole_ref[at(f, r), :]
            out_ref[at(f, r), :] = value
            new.append(coef_row(coef_ref, 0, r, f, chunks) * value)
        return tuple(new)

    def downward(s, carry):
        r = cycles - 1 - s
        new = []
        for f in range(fluids):
            gain = coef_row(coef_ref, 2, r, f, chunks)
            out_ref[at(f, r), :] = gain * (out_ref[at(f, r), :] + carry[f])
            value = carry[f] + whole_ref[at(f, r), :]
            new.append(coef_row(coef_ref, 1, r, f, chunks) * value)
        return tuple(new)

    nothing = jnp.zeros((vertical, width), jnp.float32)
    lax.fori_loop(0, cycles, upward, (nothing,) * fluids)
    lax.fori_loop(0, cycles, downward, (nothing,) * fluids)


def scans(coef, whole, vertical, fluids):
    return pl.pallas_call(
        functools.partial(scan_kernel, vertical, fluids),
        out_shape=jax.ShapeDtypeStruct(whole.shape, jnp.float32),
        compiler_params=params(),
        cost_estimate=cost(0, 3 * whole.size * 4),
    )(coef, whole)


def finish_kernel(vertical, fluids, groups, coef_ref, link_ref, local_ref, *refs):
    in_refs = refs[: groups - 1]
    (out_ref,) = refs[groups - 1 :]
    width = local_ref.shape[1]
    cycles = local_ref.shape[0] // vertical // fluids
    chunks = width // LANES
    entering = []
    for f in range(fluids):
        for way in range(2):
            value = jnp.zeros((vertical, width), jnp.float32)
            for step in range(groups - 1):
                factor = link_ref[2 * step + way, 0:1, f * LANES : (f + 1) * LANES]
                value = value + jnp.tile(factor, (1, chunks)) * in_refs[step][f]
            entering.append(value)

    def one_cycle(r, carry):
        for f in range(fluids):
            at = pl.ds(pl.multiple_of((f * cycles + r) * vertical, vertical), vertical)
            out_ref[at, :] = (
                local_ref[at, :]
                + coef_row(coef_ref, 3, r, f, chunks) * entering[2 * f]
                + coef_row(coef_ref, 4, r, f, chunks) * entering[2 * f + 1]
            )
        return carry

    lax.fori_loop(0, cycles, one_cycle, 0)


def finish(coef, links, local, arrived, vertical, fluids):
    groups = len(arrived) + 1
    return pl.pallas_call(
        functools.partial(finish_kernel, vertical, fluids, groups),
        out_shape=jax.ShapeDtypeStruct(local.shape, jnp.float32),
        compiler_params=params(),
        cost_estimate=cost(0, 2 * local.size * 4),
    )(coef, links, local, *arrived)


def per_device(fields, cycle_blocks, cycle_cells, cycle_fracs, coupling):
    fluids, cycles, vertical, width = fields.shape
    devices = lax.axis_size("az")
    groups = lax.axis_size("rad")
    rank = lax.axis_index("rad")
    ends = [partner_of(rank, step, groups) for step in range(1, groups)]
    ranks = jnp.stack([rank] + [e[1] for e in ends] + [e[0] for e in ends]).astype(jnp.int32)

    messages = spread(fields.reshape(fluids * cycles * vertical, width), vertical)
    slices = [messages[0]] + [sent_along(messages[z], "az", z) for z in range(1, vertical)]
    tail = messages[vertical]
    if devices > vertical:
        tail = sent_along(tail, "az", vertical)
    others = [exchanged(coupling, "rad", step) for step in range(1, groups)]
    coef, links = coefficients(coupling, ranks, others)

    pieces = turn(slices, tail, cycle_blocks, cycle_cells, cycle_fracs, fluids, width, devices)
    placed = [pieces[0]] + [sent_along(pieces[e], "az", devices - e) for e in range(1, devices)]
    whole, *ends_out = gather(
        placed, cycle_blocks, cycle_cells, ranks, coef, fluids, vertical, groups
    )
    arrived = [exchanged(ends_out[step - 1], "rad", step) for step in range(1, groups)]
    local = scans(coef, whole, vertical, fluids)
    solved = finish(coef, links, local, arrived, vertical, fluids)
    return solved.reshape(fields.shape)


def solution(mesh):
    return jax.shard_map(
        per_device,
        mesh=mesh,
        in_specs=(P(None, "rad", None, "az"), P("rad", None), P("rad"), P("rad"), P(None, "rad")),
        out_specs=P(None, "rad", None, "az"),
        check_vma=False,
    )
```

```python
import functools

import jax
import jax.numpy as jnp
from jax import lax
from jax.experimental import pallas as pl
from jax.experimental.pallas import tpu as pltpu
from jax.sharding import PartitionSpec as P

LANES = 128
SUBLANES = 8
VMEM_LIMIT = 24 * 1024 * 1024


def smem():
    return pl.BlockSpec(memory_space=pltpu.SMEM)


def params():
    return pltpu.CompilerParams(vmem_limit_bytes=VMEM_LIMIT)


def cost(flops, moved):
    return pl.CostEstimate(flops=flops, bytes_accessed=moved, transcendentals=0)


def sent_along(block, axis, distance):
    size = lax.axis_size(axis)
    return lax.ppermute(block, axis, [(i, (i + distance) % size) for i in range(size)])


def along_all(blocks, axis, distances):
    size = lax.axis_size(axis)
    order = sorted(distances, key=lambda i: min(distances[i], size - distances[i]), reverse=True)
    sent = {i: sent_along(blocks[i], axis, distances[i]) if distances[i] else blocks[i] for i in order}
    return [sent[i] for i in range(len(blocks))]


def partner_of(rank, step, size):
    if size & (size - 1) == 0:
        return rank ^ step, rank ^ step
    return (rank + step) % size, (rank - step) % size


def exchanged(block, axis, step):
    size = lax.axis_size(axis)
    return lax.ppermute(block, axis, [(i, partner_of(i, step, size)[0]) for i in range(size)])


def spread_kernel(vertical, x_ref, pass_ref, *refs):
    out_refs, (passed_ref, held, sems) = refs[:-3], refs[-3:]
    passed_ref[...] = pass_ref[...]
    chunks, rows = held.shape[0], held.shape[1] // vertical
    copies = [
        pltpu.make_async_copy(x_ref.at[:, q * LANES : (q + 1) * LANES], held.at[q], sems.at[q])
        for q in range(chunks)
    ]
    for copy in copies:
        copy.start()
    lane = lax.broadcasted_iota(jnp.int32, (SUBLANES, LANES), 1)
    for q in range(chunks):
        copies[q].wait()
        for z in range(vertical):
            out_refs[z][q * rows : (q + 1) * rows, :] = held[q, pl.ds(z, rows, stride=vertical), :]
    out_refs[0][chunks * rows :, :] = jnp.zeros((SUBLANES, LANES), jnp.float32)
    for z in range(vertical):
        tile = jnp.zeros((SUBLANES, LANES), jnp.float32)
        for g in range(rows // SUBLANES):
            start = (chunks - 1) * rows + g * SUBLANES
            last = out_refs[z][start : start + SUBLANES, :]
            tile = jnp.where(lane == g, pltpu.roll(last, g + 1, 1), tile)
        if z + 1 < vertical:
            out_refs[z + 1][chunks * rows :, :] = tile
        else:
            out_refs[vertical][...] = tile


def spread(x, passed, vertical):
    total, width = x.shape
    rows = total // vertical
    main = jax.ShapeDtypeStruct((rows * width // LANES + SUBLANES, LANES), jnp.float32)
    tail = jax.ShapeDtypeStruct((SUBLANES, LANES), jnp.float32)
    chunks = width // LANES
    return pl.pallas_call(
        functools.partial(spread_kernel, vertical),
        out_shape=[main] * vertical + [tail, jax.ShapeDtypeStruct(passed.shape, passed.dtype)],
        in_specs=[pl.BlockSpec(memory_space=pl.ANY), pl.BlockSpec()],
        scratch_shapes=[
            pltpu.VMEM((chunks, total, LANES), jnp.float32),
            pltpu.SemaphoreType.DMA((chunks,)),
        ],
        compiler_params=params(),
        cost_estimate=cost(0, 2 * total * width * 4),
    )(x, passed)


def turn_kernel(vertical, devices, fluids, awaited, blocks, cells, fracs, *refs):
    refs = refs[awaited:]
    in_refs = refs[:vertical]
    tail_ref = refs[vertical]
    out_refs = refs[vertical + 1 : vertical + 1 + devices]
    held, edge, sorted_ref = refs[vertical + 1 + devices :]
    chunks, rows = held.shape[0], held.shape[1] // vertical
    width = chunks * LANES
    cycles = rows // fluids
    for z in range(vertical):
        for q in range(chunks):
            held[q, pl.ds(z, rows, stride=vertical), :] = in_refs[z][q * rows : (q + 1) * rows, :]
        if z + 1 < vertical:
            tile = in_refs[z + 1][chunks * rows :, :]
        else:
            tile = tail_ref[...]
        for g in range(rows // SUBLANES):
            turned = tile if g == 0 else pltpu.roll(tile, LANES - g, 1)
            edge[pl.ds(z + g * SUBLANES * vertical, SUBLANES, stride=vertical), :] = turned
    lane = lax.broadcasted_iota(jnp.int32, (vertical, width), 1)
    wide_lane = lax.broadcasted_iota(jnp.int32, (devices, width), 1)

    def one_cycle(r, carry):
        shift = cells[r]
        block = blocks[r, 0]
        weight = fracs[r]
        for f in range(fluids):
            row = f * cycles + r
            at = pl.ds(pl.multiple_of(row * vertical, vertical), vertical)
            near = jnp.concatenate([held[q, at, :] for q in range(chunks)], axis=1)
            far = jnp.where(lane == 0, edge[at, 0:1], pltpu.roll(near, 1, 1))
            mixed = (1.0 - weight) * near + weight * far
            mixed = pltpu.roll(mixed, shift, 1)
            if devices > vertical:
                pad = jnp.zeros((devices - vertical, width), jnp.float32)
                mixed = jnp.concatenate([mixed, pad], axis=0)
            first = pltpu.roll(mixed, lax.rem(devices - block, devices), 0)
            second = pltpu.roll(first, devices - 1, 0)
            to = pl.ds(pl.multiple_of(row * devices, devices), devices)
            chosen = jnp.where(wide_lane >= shift, first, second)
            for q in range(chunks):
                sorted_ref[q, to, :] = chosen[:, q * LANES : (q + 1) * LANES]
        return carry

    lax.fori_loop(0, cycles, one_cycle, 0, unroll=4)
    for e in range(devices):
        for q in range(chunks):
            out_refs[e][:, q * LANES : (q + 1) * LANES] = sorted_ref[
                q, pl.ds(e, rows, stride=devices), :
            ]


def turn(awaited, slices, tail, blocks, cells, fracs, fluids, width, devices):
    vertical = len(slices)
    cycles = cells.shape[0]
    rows = fluids * cycles
    out = jax.ShapeDtypeStruct((rows, width), jnp.float32)
    return pl.pallas_call(
        functools.partial(turn_kernel, vertical, devices, fluids, len(awaited)),
        out_shape=[out] * devices,
        in_specs=[smem()] * 3
        + [pl.BlockSpec(memory_space=pl.ANY)] * len(awaited)
        + [pl.BlockSpec()] * (vertical + 1),
        scratch_shapes=[
            pltpu.VMEM((width // LANES, rows * vertical, LANES), jnp.float32),
            pltpu.VMEM((rows * vertical, LANES), jnp.float32),
            pltpu.VMEM((width // LANES, rows * devices, LANES), jnp.float32),
        ],
        compiler_params=params(),
        cost_estimate=cost(0, 2 * rows * vertical * width * 4),
    )(blocks, cells, fracs, *awaited, *slices, tail)


def coefficient_kernel(groups, own_ref, rank_ref, *refs):
    other_refs = refs[: groups - 1]
    coef_ref, table, inner, outer = refs[groups - 1 :]
    fluids, cycles = own_ref.shape
    total = groups * cycles

    for step in range(groups):
        source = rank_ref[step]
        ref = own_ref if step == 0 else other_refs[step - 1]

        def fill(r, carry, ref=ref, source=source):
            for f in range(fluids):
                table[f, source * cycles + r] = ref[f, r]
            return carry

        lax.fori_loop(0, cycles, fill, 0, unroll=8)

    def spans(f):
        return slice(f * LANES, (f + 1) * LANES)

    one = jnp.ones((1, LANES), jnp.float32)
    for f in range(fluids):
        inner[0, :, spans(f)] = one
        outer[total - 1, :, spans(f)] = one

    def march(s, carry):
        new = []
        for f in range(fluids):
            for way in range(2):
                low, high = carry[2 * f + way]
                link = jnp.full((1, LANES), table[f, s if way == 0 else total - s], jnp.float32)
                low = low + high / link
                if way == 0:
                    inner[s, :, spans(f)] = low
                else:
                    outer[total - 1 - s, :, spans(f)] = low
                new.append((low, high + low))
        return tuple(new)

    ends = lax.fori_loop(1, total, march, ((one, one),) * (2 * fluids))
    first = rank_ref[0] * cycles
    scales = [1.0 / ends[2 * f][1] for f in range(fluids)]

    def keep(r, carry):
        for f in range(fluids):
            coef_ref[0, r, :, spans(f)] = inner[first + r, :, spans(f)]
            coef_ref[1, r, :, spans(f)] = outer[first + r, :, spans(f)] * scales[f]
        return carry

    lax.fori_loop(0, cycles, keep, 0, unroll=8)


def coefficients(own, ranks, others):
    fluids, cycles = own.shape
    groups = len(others) + 1
    total = groups * cycles
    wide = fluids * LANES
    per_cycle = pltpu.VMEM((total, 1, wide), jnp.float32)
    return pl.pallas_call(
        functools.partial(coefficient_kernel, groups),
        out_shape=jax.ShapeDtypeStruct((2, cycles, 1, wide), jnp.float32),
        in_specs=[smem()] * (groups + 1),
        scratch_shapes=[pltpu.SMEM((fluids, total), jnp.float32), per_cycle, per_cycle],
        compiler_params=params(),
        cost_estimate=cost(0, 1 << 20),
    )(own, ranks, *others)


def coef_row(coef_ref, kind, r, f, chunks):
    row = coef_ref[kind, r, :, f * LANES : (f + 1) * LANES]
    return jnp.tile(row, (1, chunks))


def gather_kernel(vertical, devices, fluids, groups, blocks, cells, ranks, coef_ref, *refs):
    in_refs = refs[:devices]
    whole_ref = refs[devices]
    send_refs = refs[devices + 1 : devices + groups]
    (arrived,) = refs[devices + groups :]
    chunks, rows = arrived.shape[0], arrived.shape[1] // devices
    width = chunks * LANES
    cycles = rows // fluids
    for e in range(devices):
        for q in range(chunks):
            arrived[q, pl.ds(e, rows, stride=devices), :] = in_refs[e][
                :, q * LANES : (q + 1) * LANES
            ]
    lane = lax.broadcasted_iota(jnp.int32, (vertical, width), 1)

    def one_cycle(r, carry):
        shift = cells[r]
        block = blocks[r, 0]
        new = []
        for f in range(fluids):
            row = f * cycles + r
            at = pl.ds(pl.multiple_of(row * devices, devices), devices)
            held = jnp.concatenate([arrived[q, at, :] for q in range(chunks)], axis=1)
            first = pltpu.roll(held, block, 0)
            second = pltpu.roll(first, 1, 0)
            value = jnp.where(lane >= shift, first[:vertical], second[:vertical])
            whole_ref[pl.ds(pl.multiple_of(row * vertical, vertical), vertical), :] = value
            new.append(carry[2 * f] + coef_row(coef_ref, 0, r, f, chunks) * value)
            new.append(carry[2 * f + 1] + coef_row(coef_ref, 1, r, f, chunks) * value)
        return tuple(new)

    nothing = jnp.zeros((vertical, width), jnp.float32)
    sums = lax.fori_loop(0, cycles, one_cycle, (nothing,) * (2 * fluids), unroll=4)
    for step in range(1, groups):
        outward = ranks[groups - 1 + step] > ranks[0]
        for f in range(fluids):
            send_refs[step - 1][f] = jnp.where(outward, sums[2 * f], sums[2 * f + 1])


def gather(pieces, blocks, cells, ranks, coef, fluids, vertical, groups):
    devices = len(pieces)
    rows, width = pieces[0].shape
    edge = jax.ShapeDtypeStruct((fluids, vertical, width), jnp.float32)
    return pl.pallas_call(
        functools.partial(gather_kernel, vertical, devices, fluids, groups),
        out_shape=[jax.ShapeDtypeStruct((rows * vertical, width), jnp.float32)]
        + [edge] * (groups - 1),
        in_specs=[smem()] * 3 + [pl.BlockSpec()] * (devices + 1),
        scratch_shapes=[pltpu.VMEM((width // LANES, rows * devices, LANES), jnp.float32)],
        compiler_params=params(),
        cost_estimate=cost(0, 2 * rows * vertical * width * 4),
    )(blocks, cells, ranks, coef, *pieces)


def scan_kernel(vertical, fluids, coef_ref, whole_ref, out_ref):
    width = whole_ref.shape[1]
    cycles = whole_ref.shape[0] // vertical // fluids
    chunks = width // LANES

    def at(f, r):
        return pl.ds(pl.multiple_of((f * cycles + r) * vertical, vertical), vertical)

    def upward(r, carry):
        new = []
        for f in range(fluids):
            total = carry[f] + coef_row(coef_ref, 0, r, f, chunks) * whole_ref[at(f, r), :]
            out_ref[at(f, r), :] = coef_row(coef_ref, 1, r, f, chunks) * total
            new.append(total)
        return tuple(new)

    def downward(s, carry):
        r = cycles - 1 - s
        new = []
        for f in range(fluids):
            out_ref[at(f, r), :] += coef_row(coef_ref, 0, r, f, chunks) * carry[f]
            new.append(carry[f] + coef_row(coef_ref, 1, r, f, chunks) * whole_ref[at(f, r), :])
        return tuple(new)

    nothing = jnp.zeros((vertical, width), jnp.float32)
    lax.fori_loop(0, cycles, upward, (nothing,) * fluids, unroll=4)
    lax.fori_loop(0, cycles, downward, (nothing,) * fluids, unroll=4)


def scans(coef, whole, vertical, fluids):
    return pl.pallas_call(
        functools.partial(scan_kernel, vertical, fluids),
        out_shape=jax.ShapeDtypeStruct(whole.shape, jnp.float32),
        compiler_params=params(),
        cost_estimate=cost(0, 3 * whole.size * 4),
    )(coef, whole)


def finish_kernel(vertical, fluids, groups, ranks, coef_ref, local_ref, *refs):
    in_refs = refs[: groups - 1]
    (out_ref,) = refs[groups - 1 :]
    width = local_ref.shape[1]
    cycles = local_ref.shape[0] // vertical // fluids
    chunks = width // LANES
    nothing = jnp.zeros((vertical, width), jnp.float32)
    entering = []
    for f in range(fluids):
        inward, outward = nothing, nothing
        for step in range(1, groups):
            value = in_refs[step - 1][f]
            from_inside = ranks[step] < ranks[0]
            inward = inward + jnp.where(from_inside, value, nothing)
            outward = outward + jnp.where(from_inside, nothing, value)
        entering += [inward, outward]

    def one_cycle(r, carry):
        for f in range(fluids):
            at = pl.ds(pl.multiple_of((f * cycles + r) * vertical, vertical), vertical)
            out_ref[at, :] = (
                local_ref[at, :]
                + coef_row(coef_ref, 1, r, f, chunks) * entering[2 * f]
                + coef_row(coef_ref, 0, r, f, chunks) * entering[2 * f + 1]
            )
        return carry

    lax.fori_loop(0, cycles, one_cycle, 0, unroll=4)


def finish(ranks, coef, local, arrived, vertical, fluids):
    groups = len(arrived) + 1
    return pl.pallas_call(
        functools.partial(finish_kernel, vertical, fluids, groups),
        out_shape=jax.ShapeDtypeStruct(local.shape, jnp.float32),
        in_specs=[smem()] + [pl.BlockSpec()] * (groups + 1),
        compiler_params=params(),
        cost_estimate=cost(0, 2 * local.size * 4),
    )(ranks, coef, local, *arrived)


def per_device(fields, cycle_blocks, cycle_cells, cycle_fracs, coupling):
    fluids, cycles, vertical, width = fields.shape
    devices = lax.axis_size("az")
    groups = lax.axis_size("rad")
    rank = lax.axis_index("rad")
    ends = [partner_of(rank, step, groups) for step in range(1, groups)]
    ranks = jnp.stack([rank] + [e[1] for e in ends] + [e[0] for e in ends]).astype(jnp.int32)

    messages = spread(fields.reshape(fluids * cycles * vertical, width), coupling, vertical)
    slices = along_all(messages[:vertical], "az", {z: z for z in range(vertical)})
    tail, own = messages[vertical:]
    if devices > vertical:
        tail = sent_along(tail, "az", vertical)
    far_first = sorted(range(1, groups), reverse=True)
    received = {step: exchanged(own, "rad", step) for step in far_first}
    others = [received[step] for step in range(1, groups)]

    pieces = turn(
        others, slices, tail, cycle_blocks, cycle_cells, cycle_fracs, fluids, width, devices
    )
    coef = coefficients(own, ranks, others)
    placed = along_all(pieces, "az", {e: (devices - e) % devices for e in range(devices)})
    whole, *ends_out = gather(
        placed, cycle_blocks, cycle_cells, ranks, coef, fluids, vertical, groups
    )
    received = {step: exchanged(ends_out[step - 1], "rad", step) for step in far_first}
    arrived = [received[step] for step in range(1, groups)]
    local = scans(coef, whole, vertical, fluids)
    solved = finish(ranks, coef, local, arrived, vertical, fluids)
    return solved.reshape(fields.shape)


def solution(mesh):
    return jax.shard_map(
        per_device,
        mesh=mesh,
        in_specs=(P(None, "rad", None, "az"), P("rad", None), P("rad"), P("rad"), P(None, "rad")),
        out_specs=P(None, "rad", None, "az"),
        check_vma=False,
    )
```

```python
import functools

import jax
import jax.numpy as jnp
from jax import lax
from jax.experimental import pallas as pl
from jax.experimental.pallas import tpu as pltpu
from jax.sharding import PartitionSpec as P

LANES = 128
SUBLANES = 8
VMEM_LIMIT = 24 * 1024 * 1024


def smem():
    return pl.BlockSpec(memory_space=pltpu.SMEM)


def params():
    return pltpu.CompilerParams(vmem_limit_bytes=VMEM_LIMIT)


def cost(flops, moved):
    return pl.CostEstimate(flops=flops, bytes_accessed=moved, transcendentals=0)


def sent_along(block, axis, distance):
    size = lax.axis_size(axis)
    return lax.ppermute(block, axis, [(i, (i + distance) % size) for i in range(size)])


def along_all(blocks, axis, distances):
    size = lax.axis_size(axis)
    order = sorted(distances, key=lambda i: min(distances[i], size - distances[i]), reverse=True)
    sent = {i: sent_along(blocks[i], axis, distances[i]) if distances[i] else blocks[i] for i in order}
    return [sent[i] for i in range(len(blocks))]


def partner_of(rank, step, size):
    if size & (size - 1) == 0:
        return rank ^ step, rank ^ step
    return (rank + step) % size, (rank - step) % size


def exchanged(block, axis, step):
    size = lax.axis_size(axis)
    return lax.ppermute(block, axis, [(i, partner_of(i, step, size)[0]) for i in range(size)])


def hbm():
    return pl.BlockSpec(memory_space=pltpu.HBM)


def spread_kernel(vertical, small, x_ref, *refs):
    small_refs, refs = refs[:small], refs[small:]
    out_refs, refs = refs[: vertical + 1], refs[vertical + 1 :]
    passed_refs, (held, sems) = refs[:small], refs[small:]
    chunks, rows = held.shape[0], held.shape[1] // vertical
    copies = [
        pltpu.make_async_copy(x_ref.at[:, q * LANES : (q + 1) * LANES], held.at[q], sems.at[q])
        for q in reversed(range(chunks))
    ]
    passing = [
        pltpu.make_async_copy(small_refs[i], passed_refs[i], sems.at[chunks + i])
        for i in range(small)
    ]
    for copy in copies + passing:
        copy.start()
    lane = lax.broadcasted_iota(jnp.int32, (SUBLANES, LANES), 1)
    out_refs[0][chunks * rows :, :] = jnp.zeros((SUBLANES, LANES), jnp.float32)
    for q in reversed(range(chunks)):
        copies[chunks - 1 - q].wait()
        for z in range(vertical):
            part = held[q, pl.ds(z, rows, stride=vertical), :]
            out_refs[z][q * rows : (q + 1) * rows, :] = part
            if q == chunks - 1:
                tile = jnp.zeros((SUBLANES, LANES), jnp.float32)
                for g in range(rows // SUBLANES):
                    last = part[g * SUBLANES : (g + 1) * SUBLANES]
                    tile = jnp.where(lane == g, pltpu.roll(last, g + 1, 1), tile)
                if z + 1 < vertical:
                    out_refs[z + 1][chunks * rows :, :] = tile
                else:
                    out_refs[vertical][...] = tile
    for copy in passing:
        copy.wait()


def spread(x, passed, vertical):
    total, width = x.shape
    rows = total // vertical
    chunks = width // LANES
    main = jax.ShapeDtypeStruct((rows * chunks + SUBLANES, LANES), jnp.float32)
    tail = jax.ShapeDtypeStruct((SUBLANES, LANES), jnp.float32)
    return pl.pallas_call(
        functools.partial(spread_kernel, vertical, len(passed)),
        out_shape=[main] * vertical
        + [tail]
        + [jax.ShapeDtypeStruct(p.shape, p.dtype) for p in passed],
        in_specs=[hbm()] * (1 + len(passed)),
        scratch_shapes=[
            pltpu.VMEM((chunks, total, LANES), jnp.float32),
            pltpu.SemaphoreType.DMA((chunks + len(passed),)),
        ],
        compiler_params=params(),
        cost_estimate=cost(0, 2 * total * width * 4),
    )(*[pltpu.with_memory_space_constraint(a, pltpu.HBM) for a in (x, *passed)])


def turn_kernel(vertical, devices, fluids, awaited, blocks, cells, fracs, *refs):
    refs = refs[awaited:]
    in_refs = refs[:vertical]
    tail_ref = refs[vertical]
    out_refs = refs[vertical + 1 : vertical + 1 + devices]
    held, edge, sorted_ref = refs[vertical + 1 + devices :]
    chunks, rows = held.shape[0], held.shape[1] // vertical
    width = chunks * LANES
    cycles = rows // fluids
    for z in range(vertical):
        for q in range(chunks):
            held[q, pl.ds(z, rows, stride=vertical), :] = in_refs[z][q * rows : (q + 1) * rows, :]
        if z + 1 < vertical:
            tile = in_refs[z + 1][chunks * rows :, :]
        else:
            tile = tail_ref[...]
        for g in range(rows // SUBLANES):
            turned = tile if g == 0 else pltpu.roll(tile, LANES - g, 1)
            edge[pl.ds(z + g * SUBLANES * vertical, SUBLANES, stride=vertical), :] = turned
    lane = lax.broadcasted_iota(jnp.int32, (vertical, width), 1)
    wide_lane = lax.broadcasted_iota(jnp.int32, (devices, width), 1)

    def one_cycle(r, carry):
        shift = cells[r]
        block = blocks[r]
        weight = fracs[r]
        for f in range(fluids):
            row = f * cycles + r
            at = pl.ds(pl.multiple_of(row * vertical, vertical), vertical)
            near = jnp.concatenate([held[q, at, :] for q in range(chunks)], axis=1)
            far = jnp.where(lane == 0, edge[at, 0:1], pltpu.roll(near, 1, 1))
            mixed = (1.0 - weight) * near + weight * far
            mixed = pltpu.roll(mixed, shift, 1)
            if devices > vertical:
                pad = jnp.zeros((devices - vertical, width), jnp.float32)
                mixed = jnp.concatenate([mixed, pad], axis=0)
            first = pltpu.roll(mixed, lax.rem(devices - block, devices), 0)
            second = pltpu.roll(first, devices - 1, 0)
            to = pl.ds(pl.multiple_of(row * devices, devices), devices)
            chosen = jnp.where(wide_lane >= shift, first, second)
            for q in range(chunks):
                sorted_ref[q, to, :] = chosen[:, q * LANES : (q + 1) * LANES]
        return carry

    lax.fori_loop(0, cycles, one_cycle, 0, unroll=4)
    for e in range(devices):
        for q in range(chunks):
            out_refs[e][:, q * LANES : (q + 1) * LANES] = sorted_ref[
                q, pl.ds(e, rows, stride=devices), :
            ]


def turn(awaited, slices, tail, blocks, cells, fracs, fluids, width, devices):
    vertical = len(slices)
    cycles = cells.shape[0]
    rows = fluids * cycles
    out = jax.ShapeDtypeStruct((rows, width), jnp.float32)
    return pl.pallas_call(
        functools.partial(turn_kernel, vertical, devices, fluids, len(awaited)),
        out_shape=[out] * devices,
        in_specs=[smem()] * 3
        + [pl.BlockSpec(memory_space=pl.ANY)] * len(awaited)
        + [pl.BlockSpec()] * (vertical + 1),
        scratch_shapes=[
            pltpu.VMEM((width // LANES, rows * vertical, LANES), jnp.float32),
            pltpu.VMEM((rows * vertical, LANES), jnp.float32),
            pltpu.VMEM((width // LANES, rows * devices, LANES), jnp.float32),
        ],
        compiler_params=params(),
        cost_estimate=cost(0, 2 * rows * vertical * width * 4),
    )(blocks, cells, fracs, *awaited, *slices, tail)


def coefficient_kernel(groups, own_ref, *refs):
    rank = lax.axis_index("rad")
    other_refs = refs[: groups - 1]
    coef_ref, table, inner, outer = refs[groups - 1 :]
    fluids, cycles = own_ref.shape
    total = groups * cycles

    for step in range(groups):
        source = partner_of(rank, step, groups)[1]
        ref = own_ref if step == 0 else other_refs[step - 1]

        def fill(r, carry, ref=ref, source=source):
            for f in range(fluids):
                table[f, source * cycles + r] = ref[f, r]
            return carry

        lax.fori_loop(0, cycles, fill, 0, unroll=8)

    def spans(f):
        return slice(f * LANES, (f + 1) * LANES)

    one = jnp.ones((1, LANES), jnp.float32)
    for f in range(fluids):
        inner[0, :, spans(f)] = one
        outer[total - 1, :, spans(f)] = one

    def march(s, carry):
        new = []
        for f in range(fluids):
            for way in range(2):
                low, high = carry[2 * f + way]
                link = jnp.full((1, LANES), table[f, s if way == 0 else total - s], jnp.float32)
                low = low + high / link
                if way == 0:
                    inner[s, :, spans(f)] = low
                else:
                    outer[total - 1 - s, :, spans(f)] = low
                new.append((low, high + low))
        return tuple(new)

    ends = lax.fori_loop(1, total, march, ((one, one),) * (2 * fluids))
    first = rank * cycles
    scales = [1.0 / ends[2 * f][1] for f in range(fluids)]

    def keep(r, carry):
        for f in range(fluids):
            coef_ref[0, r, :, spans(f)] = inner[first + r, :, spans(f)]
            coef_ref[1, r, :, spans(f)] = outer[first + r, :, spans(f)] * scales[f]
        return carry

    lax.fori_loop(0, cycles, keep, 0, unroll=8)


def coefficients(own, others):
    fluids, cycles = own.shape
    groups = len(others) + 1
    total = groups * cycles
    wide = fluids * LANES
    per_cycle = pltpu.VMEM((total, 1, wide), jnp.float32)
    return pl.pallas_call(
        functools.partial(coefficient_kernel, groups),
        out_shape=jax.ShapeDtypeStruct((2, cycles, 1, wide), jnp.float32),
        in_specs=[smem()] * groups,
        scratch_shapes=[pltpu.SMEM((fluids, total), jnp.float32), per_cycle, per_cycle],
        compiler_params=params(),
        cost_estimate=cost(0, 1 << 20),
    )(own, *others)


def coef_row(coef_ref, kind, r, f, chunks):
    row = coef_ref[kind, r, :, f * LANES : (f + 1) * LANES]
    return jnp.tile(row, (1, chunks))


def gather_kernel(vertical, devices, fluids, groups, blocks, cells, coef_ref, *refs):
    rank = lax.axis_index("rad")
    in_refs = refs[:devices]
    whole_ref = refs[devices]
    send_refs = refs[devices + 1 : devices + groups]
    (arrived,) = refs[devices + groups :]
    chunks, rows = arrived.shape[0], arrived.shape[1] // devices
    width = chunks * LANES
    cycles = rows // fluids
    for e in range(devices):
        for q in range(chunks):
            arrived[q, pl.ds(e, rows, stride=devices), :] = in_refs[e][
                :, q * LANES : (q + 1) * LANES
            ]
    lane = lax.broadcasted_iota(jnp.int32, (vertical, width), 1)

    def one_cycle(r, carry):
        shift = cells[r]
        block = blocks[r]
        new = []
        for f in range(fluids):
            row = f * cycles + r
            at = pl.ds(pl.multiple_of(row * devices, devices), devices)
            held = jnp.concatenate([arrived[q, at, :] for q in range(chunks)], axis=1)
            first = pltpu.roll(held, block, 0)
            second = pltpu.roll(first, 1, 0)
            value = jnp.where(lane >= shift, first[:vertical], second[:vertical])
            whole_ref[pl.ds(pl.multiple_of(row * vertical, vertical), vertical), :] = value
            new.append(carry[2 * f] + coef_row(coef_ref, 0, r, f, chunks) * value)
            new.append(carry[2 * f + 1] + coef_row(coef_ref, 1, r, f, chunks) * value)
        return tuple(new)

    nothing = jnp.zeros((vertical, width), jnp.float32)
    sums = lax.fori_loop(0, cycles, one_cycle, (nothing,) * (2 * fluids), unroll=4)
    for step in range(1, groups):
        outward = partner_of(rank, step, groups)[0] > rank
        for f in range(fluids):
            send_refs[step - 1][f] = jnp.where(outward, sums[2 * f], sums[2 * f + 1])


def gather(pieces, blocks, cells, coef, fluids, vertical, groups):
    devices = len(pieces)
    rows, width = pieces[0].shape
    edge = jax.ShapeDtypeStruct((fluids, vertical, width), jnp.float32)
    return pl.pallas_call(
        functools.partial(gather_kernel, vertical, devices, fluids, groups),
        out_shape=[jax.ShapeDtypeStruct((rows * vertical, width), jnp.float32)]
        + [edge] * (groups - 1),
        in_specs=[smem()] * 2 + [pl.BlockSpec()] * (devices + 1),
        scratch_shapes=[pltpu.VMEM((width // LANES, rows * devices, LANES), jnp.float32)],
        compiler_params=params(),
        cost_estimate=cost(0, 2 * rows * vertical * width * 4),
    )(blocks, cells, coef, *pieces)


def scan_kernel(vertical, fluids, coef_ref, whole_ref, out_ref):
    width = whole_ref.shape[1]
    cycles = whole_ref.shape[0] // vertical // fluids
    chunks = width // LANES

    def at(f, r):
        return pl.ds(pl.multiple_of((f * cycles + r) * vertical, vertical), vertical)

    def upward(r, carry):
        new = []
        for f in range(fluids):
            total = carry[f] + coef_row(coef_ref, 0, r, f, chunks) * whole_ref[at(f, r), :]
            out_ref[at(f, r), :] = coef_row(coef_ref, 1, r, f, chunks) * total
            new.append(total)
        return tuple(new)

    def downward(s, carry):
        r = cycles - 1 - s
        new = []
        for f in range(fluids):
            out_ref[at(f, r), :] += coef_row(coef_ref, 0, r, f, chunks) * carry[f]
            new.append(carry[f] + coef_row(coef_ref, 1, r, f, chunks) * whole_ref[at(f, r), :])
        return tuple(new)

    nothing = jnp.zeros((vertical, width), jnp.float32)
    lax.fori_loop(0, cycles, upward, (nothing,) * fluids, unroll=4)
    lax.fori_loop(0, cycles, downward, (nothing,) * fluids, unroll=4)


def scans(coef, whole, vertical, fluids):
    return pl.pallas_call(
        functools.partial(scan_kernel, vertical, fluids),
        out_shape=jax.ShapeDtypeStruct(whole.shape, jnp.float32),
        compiler_params=params(),
        cost_estimate=cost(0, 3 * whole.size * 4),
    )(coef, whole)


def finish_kernel(vertical, fluids, groups, coef_ref, local_ref, *refs):
    rank = lax.axis_index("rad")
    in_refs = refs[: groups - 1][::-1]
    (out_ref,) = refs[groups - 1 :]
    width = local_ref.shape[1]
    cycles = local_ref.shape[0] // vertical // fluids
    chunks = width // LANES
    nothing = jnp.zeros((vertical, width), jnp.float32)
    entering = []
    for f in range(fluids):
        inward, outward = nothing, nothing
        for step in range(1, groups):
            value = in_refs[step - 1][f]
            from_inside = partner_of(rank, step, groups)[1] < rank
            inward = inward + jnp.where(from_inside, value, nothing)
            outward = outward + jnp.where(from_inside, nothing, value)
        entering += [inward, outward]

    def one_cycle(r, carry):
        for f in range(fluids):
            at = pl.ds(pl.multiple_of((f * cycles + r) * vertical, vertical), vertical)
            out_ref[at, :] = (
                local_ref[at, :]
                + coef_row(coef_ref, 1, r, f, chunks) * entering[2 * f]
                + coef_row(coef_ref, 0, r, f, chunks) * entering[2 * f + 1]
            )
        return carry

    lax.fori_loop(0, cycles, one_cycle, 0, unroll=4)


def finish(coef, local, arrived, vertical, fluids):
    groups = len(arrived) + 1
    return pl.pallas_call(
        functools.partial(finish_kernel, vertical, fluids, groups),
        out_shape=jax.ShapeDtypeStruct(local.shape, jnp.float32),
        compiler_params=params(),
        cost_estimate=cost(0, 2 * local.size * 4),
    )(coef, local, *arrived[::-1])


def per_device(fields, cycle_blocks, cycle_cells, cycle_fracs, coupling):
    fluids, cycles, vertical, width = fields.shape
    devices = lax.axis_size("az")
    groups = lax.axis_size("rad")
    small = (coupling, cycle_blocks.reshape(cycles), cycle_cells, cycle_fracs)
    messages = spread(fields.reshape(fluids * cycles * vertical, width), small, vertical)
    slices = along_all(messages[:vertical], "az", {z: z for z in range(vertical)})
    tail, own, blocks, cells, fracs = messages[vertical:]
    if devices > vertical:
        tail = sent_along(tail, "az", vertical)
    far_first = sorted(range(1, groups), reverse=True)
    received = {step: exchanged(own, "rad", step) for step in far_first}
    others = [received[step] for step in range(1, groups)]

    pieces = turn(others, slices, tail, blocks, cells, fracs, fluids, width, devices)
    coef = coefficients(own, others)
    placed = along_all(pieces, "az", {e: (devices - e) % devices for e in range(devices)})
    whole, *ends_out = gather(placed, blocks, cells, coef, fluids, vertical, groups)
    received = {step: exchanged(ends_out[step - 1], "rad", step) for step in far_first}
    arrived = [received[step] for step in range(1, groups)]
    local = scans(coef, whole, vertical, fluids)
    solved = finish(coef, local, arrived, vertical, fluids)
    return solved.reshape(fields.shape)


def solution(mesh):
    return jax.shard_map(
        per_device,
        mesh=mesh,
        in_specs=(P(None, "rad", None, "az"), P("rad", None), P("rad"), P("rad"), P(None, "rad")),
        out_specs=P(None, "rad", None, "az"),
        check_vma=False,
    )
```

```python
import functools

import jax
import jax.numpy as jnp
from jax import lax
from jax.experimental import pallas as pl
from jax.experimental.pallas import tpu as pltpu
from jax.sharding import PartitionSpec as P

LANES = 128
SUBLANES = 8
VMEM_LIMIT = 24 * 1024 * 1024
OUT_PARTS = 4


def smem():
    return pl.BlockSpec(memory_space=pltpu.SMEM)


def params():
    return pltpu.CompilerParams(vmem_limit_bytes=VMEM_LIMIT)


def cost(flops, moved):
    return pl.CostEstimate(flops=flops, bytes_accessed=moved, transcendentals=0)


def sent_along(block, axis, distance):
    size = lax.axis_size(axis)
    return lax.ppermute(block, axis, [(i, (i + distance) % size) for i in range(size)])


def along_all(blocks, axis, distances):
    return [sent_along(b, axis, d) if d else b for b, d in zip(blocks, distances)]


def first_order(count):
    return sorted(range(count), key=lambda z: (z % 2, -z))


def second_order(count):
    return sorted(range(count), key=lambda e: (count - e) % count)


def restored(refs, order):
    return [refs[order.index(i)] for i in range(len(order))]


def partner_of(rank, step, size):
    if size & (size - 1) == 0:
        return rank ^ step, rank ^ step
    return (rank + step) % size, (rank - step) % size


def exchanged(block, axis, step):
    size = lax.axis_size(axis)
    return lax.ppermute(block, axis, [(i, partner_of(i, step, size)[0]) for i in range(size)])


def hbm():
    return pl.BlockSpec(memory_space=pltpu.HBM)


def spread_kernel(vertical, small, x_ref, *refs):
    small_refs, refs = refs[:small], refs[small:]
    out_refs, refs = refs[: vertical + 1], refs[vertical + 1 :]
    passed_refs, (held, sems) = refs[:small], refs[small:]
    chunks, rows = held.shape[0], held.shape[1] // vertical
    copies = [
        pltpu.make_async_copy(x_ref.at[:, q * LANES : (q + 1) * LANES], held.at[q], sems.at[q])
        for q in reversed(range(chunks))
    ]
    passing = [
        pltpu.make_async_copy(small_refs[i], passed_refs[i], sems.at[chunks + i])
        for i in range(small)
    ]
    for copy in copies + passing:
        copy.start()
    lane = lax.broadcasted_iota(jnp.int32, (SUBLANES, LANES), 1)
    out_refs[0][chunks * rows :, :] = jnp.zeros((SUBLANES, LANES), jnp.float32)
    for q in reversed(range(chunks)):
        copies[chunks - 1 - q].wait()
        for z in range(vertical):
            part = held[q, pl.ds(z, rows, stride=vertical), :]
            out_refs[z][q * rows : (q + 1) * rows, :] = part
            if q == chunks - 1:
                tile = jnp.zeros((SUBLANES, LANES), jnp.float32)
                for g in range(rows // SUBLANES):
                    last = part[g * SUBLANES : (g + 1) * SUBLANES]
                    tile = jnp.where(lane == g, pltpu.roll(last, g + 1, 1), tile)
                if z + 1 < vertical:
                    out_refs[z + 1][chunks * rows :, :] = tile
                else:
                    out_refs[vertical][...] = tile
    for copy in passing:
        copy.wait()


def spread(x, passed, vertical):
    total, width = x.shape
    rows = total // vertical
    chunks = width // LANES
    main = jax.ShapeDtypeStruct((rows * chunks + SUBLANES, LANES), jnp.float32)
    tail = jax.ShapeDtypeStruct((SUBLANES, LANES), jnp.float32)
    return pl.pallas_call(
        functools.partial(spread_kernel, vertical, len(passed)),
        out_shape=[main] * vertical
        + [tail]
        + [jax.ShapeDtypeStruct(p.shape, p.dtype) for p in passed],
        in_specs=[hbm()] * (1 + len(passed)),
        scratch_shapes=[
            pltpu.VMEM((chunks, total, LANES), jnp.float32),
            pltpu.SemaphoreType.DMA((chunks + len(passed),)),
        ],
        compiler_params=params(),
        cost_estimate=cost(0, 2 * total * width * 4),
    )(*[pltpu.with_memory_space_constraint(a, pltpu.HBM) for a in (x, *passed)])


def turn_kernel(vertical, devices, fluids, awaited, *refs):
    tables, refs = refs[:3], refs[3 + awaited :]
    in_refs = restored(refs[:vertical], first_order(vertical))
    tail_ref = refs[vertical]
    out_refs = refs[vertical + 1 : vertical + 1 + devices]
    blocks, cells, fracs, held, edge, sorted_ref, sems = refs[vertical + 1 + devices :]
    chunks, rows = held.shape[0], held.shape[1] // vertical
    cycles = rows // fluids
    copies = [
        pltpu.make_async_copy(table, scalars, sems.at[i])
        for i, (table, scalars) in enumerate(zip(tables, (blocks, cells, fracs)))
    ]
    for copy in copies:
        copy.start()
    for z in range(vertical):
        for q in range(chunks):
            held[q, pl.ds(z, rows, stride=vertical), :] = in_refs[z][q * rows : (q + 1) * rows, :]
        if z + 1 < vertical:
            tile = in_refs[z + 1][chunks * rows :, :]
        else:
            tile = tail_ref[...]
        for g in range(rows // SUBLANES):
            turned = tile if g == 0 else pltpu.roll(tile, LANES - g, 1)
            edge[pl.ds(z + g * SUBLANES * vertical, SUBLANES, stride=vertical), :] = turned
    for copy in copies:
        copy.wait()
    lane = lax.broadcasted_iota(jnp.int32, (vertical, LANES), 1)
    tall_lane = lax.broadcasted_iota(jnp.int32, (devices, LANES), 1)

    def one_cycle(r, carry):
        whole, part = cells[r] // LANES, lax.rem(cells[r], LANES)
        turn_by = lax.rem(devices - blocks[r], devices)
        weight = fracs[r]
        inside = tall_lane < part
        for f in range(fluids):
            row = f * cycles + r
            at = pl.ds(pl.multiple_of(row * vertical, vertical), vertical)
            near = [held[q, at, :] for q in range(chunks)]
            moved = [pltpu.roll(x, 1, 1) for x in near]
            turned = []
            for q in range(chunks):
                far = jnp.where(lane == 0, moved[q - 1] if q else edge[at, :], moved[q])
                mixed = pltpu.roll((1.0 - weight) * near[q] + weight * far, part, 1)
                if devices > vertical:
                    pad = jnp.zeros((devices - vertical, LANES), jnp.float32)
                    mixed = jnp.concatenate([mixed, pad], axis=0)
                turned.append(pltpu.roll(mixed, turn_by, 0))
            to = pl.ds(pl.multiple_of(row * devices, devices), devices)
            for q in range(chunks):
                if q == 0:
                    around = pltpu.roll(turned[chunks - 1], devices - 1, 0)
                    value = jnp.where(inside, around, turned[0])
                else:
                    value = jnp.where(inside, turned[q - 1], turned[q])
                    value = jnp.where(
                        whole + q >= chunks, pltpu.roll(value, devices - 1, 0), value
                    )
                sorted_ref[lax.rem(whole + q, chunks), to, :] = value
        return carry

    lax.fori_loop(0, cycles, one_cycle, 0, unroll=8)
    for e in range(devices):
        for q in range(chunks):
            out_refs[e][:, q * LANES : (q + 1) * LANES] = sorted_ref[
                q, pl.ds(e, rows, stride=devices), :
            ]


def vmem():
    return pl.BlockSpec(memory_space=pltpu.VMEM)


def turn(awaited, slices, tail, blocks, cells, fracs, fluids, width, devices):
    vertical = len(slices)
    cycles = cells.shape[0]
    rows = fluids * cycles
    out = jax.ShapeDtypeStruct((rows, width), jnp.float32)
    return pl.pallas_call(
        functools.partial(turn_kernel, vertical, devices, fluids, len(awaited)),
        out_shape=[out] * devices,
        in_specs=[pl.BlockSpec(memory_space=pl.ANY)] * (3 + len(awaited))
        + [vmem()] * (vertical + 1),
        scratch_shapes=[
            pltpu.SMEM((cycles,), jnp.int32),
            pltpu.SMEM((cycles,), jnp.int32),
            pltpu.SMEM((cycles,), jnp.float32),
            pltpu.VMEM((width // LANES, rows * vertical, LANES), jnp.float32),
            pltpu.VMEM((rows * vertical, LANES), jnp.float32),
            pltpu.VMEM((width // LANES, rows * devices, LANES), jnp.float32),
            pltpu.SemaphoreType.DMA((3,)),
        ],
        compiler_params=params(),
        cost_estimate=cost(0, 2 * rows * vertical * width * 4),
    )(blocks, cells, fracs, *awaited, *[slices[i] for i in first_order(vertical)], tail)


def coefficient_kernel(groups, own_ref, *refs):
    rank = lax.axis_index("rad")
    other_refs = refs[: groups - 1]
    coef_ref, table, inner, outer = refs[groups - 1 :]
    fluids, cycles = own_ref.shape
    total = groups * cycles

    for step in range(groups):
        source = partner_of(rank, step, groups)[1]
        ref = own_ref if step == 0 else other_refs[step - 1]

        def fill(r, carry, ref=ref, source=source):
            for f in range(fluids):
                table[f, source * cycles + r] = ref[f, r]
            return carry

        lax.fori_loop(0, cycles, fill, 0, unroll=8)

    def spans(f):
        return slice(f * LANES, (f + 1) * LANES)

    one = jnp.ones((1, LANES), jnp.float32)
    for f in range(fluids):
        inner[0, :, spans(f)] = one
        outer[total - 1, :, spans(f)] = one

    def march(s, carry):
        new = []
        for f in range(fluids):
            for way in range(2):
                low, high = carry[2 * f + way]
                link = jnp.full((1, LANES), table[f, s if way == 0 else total - s], jnp.float32)
                low = low + high / link
                if way == 0:
                    inner[s, :, spans(f)] = low
                else:
                    outer[total - 1 - s, :, spans(f)] = low
                new.append((low, high + low))
        return tuple(new)

    ends = lax.fori_loop(1, total, march, ((one, one),) * (2 * fluids))
    first = rank * cycles
    scales = [1.0 / ends[2 * f][1] for f in range(fluids)]

    def keep(r, carry):
        for f in range(fluids):
            coef_ref[0, r, :, spans(f)] = inner[first + r, :, spans(f)]
            coef_ref[1, r, :, spans(f)] = outer[first + r, :, spans(f)] * scales[f]
        return carry

    lax.fori_loop(0, cycles, keep, 0, unroll=8)


def coefficients(own, others):
    fluids, cycles = own.shape
    groups = len(others) + 1
    total = groups * cycles
    wide = fluids * LANES
    per_cycle = pltpu.VMEM((total, 1, wide), jnp.float32)
    return pl.pallas_call(
        functools.partial(coefficient_kernel, groups),
        out_shape=jax.ShapeDtypeStruct((2, cycles, 1, wide), jnp.float32),
        in_specs=[smem()] * groups,
        scratch_shapes=[pltpu.SMEM((fluids, total), jnp.float32), per_cycle, per_cycle],
        compiler_params=params(),
        cost_estimate=cost(0, 1 << 20),
    )(own, *others)


def coef_row(coef_ref, kind, r, f, chunks):
    row = coef_ref[kind, r, :, f * LANES : (f + 1) * LANES]
    return jnp.tile(row, (1, chunks))


def gather_kernel(vertical, devices, fluids, groups, block_table, cell_table, coef_ref, *refs):
    rank = lax.axis_index("rad")
    in_refs = restored(refs[:devices], second_order(devices))
    whole_ref = refs[devices]
    send_refs = refs[devices + 1 : devices + groups]
    blocks, cells, arrived, sems = refs[devices + groups :]
    copies = [
        pltpu.make_async_copy(block_table, blocks, sems.at[0]),
        pltpu.make_async_copy(cell_table, cells, sems.at[1]),
    ]
    for copy in copies:
        copy.start()
    chunks, rows = arrived.shape[0], arrived.shape[1] // devices
    width = chunks * LANES
    cycles = rows // fluids
    for e in range(devices):
        for q in range(chunks):
            arrived[q, pl.ds(e, rows, stride=devices), :] = in_refs[e][
                :, q * LANES : (q + 1) * LANES
            ]
    for copy in copies:
        copy.wait()
    lane = lax.broadcasted_iota(jnp.int32, (vertical, width), 1)

    def one_cycle(r, carry):
        shift = cells[r]
        block = blocks[r]
        new = []
        for f in range(fluids):
            row = f * cycles + r
            at = pl.ds(pl.multiple_of(row * devices, devices), devices)
            held = jnp.concatenate([arrived[q, at, :] for q in range(chunks)], axis=1)
            first = pltpu.roll(held, block, 0)
            second = pltpu.roll(first, 1, 0)
            value = jnp.where(lane >= shift, first[:vertical], second[:vertical])
            whole_ref[pl.ds(pl.multiple_of(row * vertical, vertical), vertical), :] = value
            new.append(carry[2 * f] + coef_row(coef_ref, 0, r, f, chunks) * value)
            new.append(carry[2 * f + 1] + coef_row(coef_ref, 1, r, f, chunks) * value)
        return tuple(new)

    nothing = jnp.zeros((vertical, width), jnp.float32)
    sums = lax.fori_loop(0, cycles, one_cycle, (nothing,) * (2 * fluids), unroll=4)
    for step in range(1, groups):
        outward = partner_of(rank, step, groups)[0] > rank
        for f in range(fluids):
            send_refs[step - 1][f] = jnp.where(outward, sums[2 * f], sums[2 * f + 1])


def gather(pieces, blocks, cells, coef, fluids, vertical, groups):
    devices = len(pieces)
    rows, width = pieces[0].shape
    edge = jax.ShapeDtypeStruct((fluids, vertical, width), jnp.float32)
    return pl.pallas_call(
        functools.partial(gather_kernel, vertical, devices, fluids, groups),
        out_shape=[jax.ShapeDtypeStruct((rows * vertical, width), jnp.float32)]
        + [edge] * (groups - 1),
        in_specs=[pl.BlockSpec(memory_space=pl.ANY)] * 2 + [vmem()] * (devices + 1),
        scratch_shapes=[
            pltpu.SMEM(blocks.shape, jnp.int32),
            pltpu.SMEM(cells.shape, jnp.int32),
            pltpu.VMEM((width // LANES, rows * devices, LANES), jnp.float32),
            pltpu.SemaphoreType.DMA((2,)),
        ],
        compiler_params=params(),
        cost_estimate=cost(0, 2 * rows * vertical * width * 4),
    )(blocks, cells, coef, *[pieces[i] for i in second_order(devices)])


def scan_kernel(vertical, fluids, coef_ref, whole_ref, out_ref):
    width = whole_ref.shape[1]
    cycles = whole_ref.shape[0] // vertical // fluids
    chunks = width // LANES

    def at(f, r):
        return pl.ds(pl.multiple_of((f * cycles + r) * vertical, vertical), vertical)

    def upward(r, carry):
        new = []
        for f in range(fluids):
            total = carry[f] + coef_row(coef_ref, 0, r, f, chunks) * whole_ref[at(f, r), :]
            out_ref[at(f, r), :] = coef_row(coef_ref, 1, r, f, chunks) * total
            new.append(total)
        return tuple(new)

    def downward(s, carry):
        r = cycles - 1 - s
        new = []
        for f in range(fluids):
            out_ref[at(f, r), :] += coef_row(coef_ref, 0, r, f, chunks) * carry[f]
            new.append(carry[f] + coef_row(coef_ref, 1, r, f, chunks) * whole_ref[at(f, r), :])
        return tuple(new)

    nothing = jnp.zeros((vertical, width), jnp.float32)
    lax.fori_loop(0, cycles, upward, (nothing,) * fluids, unroll=4)
    lax.fori_loop(0, cycles, downward, (nothing,) * fluids, unroll=4)


def scans(coef, whole, vertical, fluids):
    return pl.pallas_call(
        functools.partial(scan_kernel, vertical, fluids),
        out_shape=jax.ShapeDtypeStruct(whole.shape, jnp.float32),
        compiler_params=params(),
        cost_estimate=cost(0, 3 * whole.size * 4),
    )(coef, whole)


def finish_kernel(vertical, fluids, groups, coef_ref, local_ref, *refs):
    rank = lax.axis_index("rad")
    in_refs = refs[: groups - 1][::-1]
    out_ref, done, sems = refs[groups - 1 :]
    width = local_ref.shape[1]
    cycles = local_ref.shape[0] // vertical // fluids
    chunks = width // LANES
    nothing = jnp.zeros((vertical, width), jnp.float32)
    entering = []
    for f in range(fluids):
        inward, outward = nothing, nothing
        for step in range(1, groups):
            value = in_refs[step - 1][f]
            from_inside = partner_of(rank, step, groups)[1] < rank
            inward = inward + jnp.where(from_inside, value, nothing)
            outward = outward + jnp.where(from_inside, nothing, value)
        entering += [inward, outward]

    parts = sems.shape[0]
    size = cycles // parts

    def copy_of(f, part):
        at = pl.ds((f * cycles + part * size) * vertical, size * vertical)
        return pltpu.make_async_copy(done.at[at], out_ref.at[at], sems.at[part, f])

    def one_cycle(r, carry):
        for f in range(fluids):
            at = pl.ds(pl.multiple_of((f * cycles + r) * vertical, vertical), vertical)
            done[at, :] = (
                local_ref[at, :]
                + coef_row(coef_ref, 1, r, f, chunks) * entering[2 * f]
                + coef_row(coef_ref, 0, r, f, chunks) * entering[2 * f + 1]
            )
        return carry

    for part in range(parts):
        lax.fori_loop(part * size, (part + 1) * size, one_cycle, 0, unroll=4)
        for f in range(fluids):
            copy_of(f, part).start()
    for part in range(parts):
        for f in range(fluids):
            copy_of(f, part).wait()


def finish(coef, local, arrived, vertical, fluids):
    groups = len(arrived) + 1
    return pl.pallas_call(
        functools.partial(finish_kernel, vertical, fluids, groups),
        out_shape=jax.ShapeDtypeStruct(local.shape, jnp.float32),
        in_specs=[vmem()] * (groups + 1),
        out_specs=hbm(),
        scratch_shapes=[
            pltpu.VMEM(local.shape, jnp.float32),
            pltpu.SemaphoreType.DMA((OUT_PARTS, fluids)),
        ],
        compiler_params=params(),
        cost_estimate=cost(0, 2 * local.size * 4),
    )(coef, local, *arrived[::-1])


def per_device(fields, cycle_blocks, cycle_cells, cycle_fracs, coupling):
    fluids, cycles, vertical, width = fields.shape
    devices = lax.axis_size("az")
    groups = lax.axis_size("rad")
    small = (coupling, cycle_blocks.reshape(cycles), cycle_cells, cycle_fracs)
    messages = spread(fields.reshape(fluids * cycles * vertical, width), small, vertical)
    slices = along_all(messages[:vertical], "az", range(vertical))
    tail, own, blocks, cells, fracs = messages[vertical:]
    if devices > vertical:
        tail = sent_along(tail, "az", vertical)
    far_first = sorted(range(1, groups), reverse=True)
    received = {step: exchanged(own, "rad", step) for step in far_first}
    others = [received[step] for step in range(1, groups)]

    pieces = turn(others, slices, tail, blocks, cells, fracs, fluids, width, devices)
    coef = coefficients(own, others)
    placed = along_all(pieces, "az", [(devices - e) % devices for e in range(devices)])
    whole, *ends_out = gather(placed, blocks, cells, coef, fluids, vertical, groups)
    received = {step: exchanged(ends_out[step - 1], "rad", step) for step in far_first}
    arrived = [received[step] for step in range(1, groups)]
    local = scans(coef, whole, vertical, fluids)
    solved = finish(coef, local, arrived, vertical, fluids)
    return solved.reshape(fields.shape)


def solution(mesh):
    return jax.shard_map(
        per_device,
        mesh=mesh,
        in_specs=(P(None, "rad", None, "az"), P("rad", None), P("rad"), P("rad"), P(None, "rad")),
        out_specs=P(None, "rad", None, "az"),
        check_vma=False,
    )
```

```python
import functools

import jax
import jax.numpy as jnp
from jax import lax
from jax.experimental import pallas as pl
from jax.experimental.pallas import tpu as pltpu
from jax.sharding import PartitionSpec as P

LANE_BITS = 7
LANES = 1 << LANE_BITS
SUBLANES = 8
VMEM_LIMIT = 24 * 1024 * 1024
OUT_PARTS = 4


def smem():
    return pl.BlockSpec(memory_space=pltpu.SMEM)


def params():
    return pltpu.CompilerParams(vmem_limit_bytes=VMEM_LIMIT)


def cost(flops, moved):
    return pl.CostEstimate(flops=flops, bytes_accessed=moved, transcendentals=0)


def sent_along(block, axis, distance):
    size = lax.axis_size(axis)
    return lax.ppermute(block, axis, [(i, (i + distance) % size) for i in range(size)])


def along_all(blocks, axis, distances):
    return [sent_along(b, axis, d) if d else b for b, d in zip(blocks, distances)]


def first_order(count):
    half = count // 2
    return sorted(range(count), key=lambda z: (z % 2, (1 - z % 2 * 2) * abs(z - half), -z))


def second_order(count):
    return sorted(range(count), key=lambda e: (count - e) % count)


def restored(refs, order):
    return [refs[order.index(i)] for i in range(len(order))]


def partner_of(rank, step, size):
    if size & (size - 1) == 0:
        return rank ^ step, rank ^ step
    return (rank + step) % size, (rank - step) % size


def exchanged(block, axis, step):
    size = lax.axis_size(axis)
    return lax.ppermute(block, axis, [(i, partner_of(i, step, size)[0]) for i in range(size)])


def hbm():
    return pl.BlockSpec(memory_space=pltpu.HBM)


def spread_kernel(vertical, small, x_ref, *refs):
    small_refs, refs = refs[:small], refs[small:]
    out_refs, refs = refs[: vertical + 1], refs[vertical + 1 :]
    passed_refs, (held, sems) = refs[:small], refs[small:]
    chunks, rows = held.shape[0], held.shape[1] // vertical
    copies = [
        pltpu.make_async_copy(x_ref.at[:, q * LANES : (q + 1) * LANES], held.at[q], sems.at[q])
        for q in reversed(range(chunks))
    ]
    passing = [
        pltpu.make_async_copy(small_refs[i], passed_refs[i], sems.at[chunks + i])
        for i in range(small)
    ]
    for copy in copies + passing:
        copy.start()
    lane = lax.broadcasted_iota(jnp.int32, (SUBLANES, LANES), 1)
    out_refs[0][chunks * rows :, :] = jnp.zeros((SUBLANES, LANES), jnp.float32)
    for q in reversed(range(chunks)):
        copies[chunks - 1 - q].wait()
        for z in range(vertical):
            part = held[q, pl.ds(z, rows, stride=vertical), :]
            out_refs[z][q * rows : (q + 1) * rows, :] = part
            if q == chunks - 1:
                tile = jnp.zeros((SUBLANES, LANES), jnp.float32)
                for g in range(rows // SUBLANES):
                    last = part[g * SUBLANES : (g + 1) * SUBLANES]
                    tile = jnp.where(lane == g, pltpu.roll(last, g + 1, 1), tile)
                if z + 1 < vertical:
                    out_refs[z + 1][chunks * rows :, :] = tile
                else:
                    out_refs[vertical][...] = tile
    for copy in passing:
        copy.wait()


def spread(x, passed, vertical):
    total, width = x.shape
    rows = total // vertical
    chunks = width // LANES
    main = jax.ShapeDtypeStruct((rows * chunks + SUBLANES, LANES), jnp.float32)
    tail = jax.ShapeDtypeStruct((SUBLANES, LANES), jnp.float32)
    return pl.pallas_call(
        functools.partial(spread_kernel, vertical, len(passed)),
        out_shape=[main] * vertical
        + [tail]
        + [jax.ShapeDtypeStruct(p.shape, p.dtype) for p in passed],
        in_specs=[hbm()] * (1 + len(passed)),
        scratch_shapes=[
            pltpu.VMEM((chunks, total, LANES), jnp.float32),
            pltpu.SemaphoreType.DMA((chunks + len(passed),)),
        ],
        compiler_params=params(),
        cost_estimate=cost(0, 2 * total * width * 4),
    )(*[pltpu.with_memory_space_constraint(a, pltpu.HBM) for a in (x, *passed)])


def turn_kernel(vertical, devices, fluids, awaited, *refs):
    tables, refs = refs[:3], refs[3 + awaited :]
    in_refs = restored(refs[:vertical], first_order(vertical))
    tail_ref = refs[vertical]
    out_refs = refs[vertical + 1 : vertical + 1 + devices]
    blocks, cells, fracs, held, edge, sorted_ref, sems = refs[vertical + 1 + devices :]
    chunks, rows = held.shape[0], held.shape[1] // vertical
    cycles = rows // fluids
    copies = [
        pltpu.make_async_copy(table, scalars, sems.at[i])
        for i, (table, scalars) in enumerate(zip(tables, (blocks, cells, fracs)))
    ]
    for copy in copies:
        copy.start()
    def place(q, carry):
        at = pl.ds(pl.multiple_of(q * rows, rows), rows)
        for z in range(vertical):
            held[q, pl.ds(z, rows, stride=vertical), :] = in_refs[z][at, :]
        return carry

    lax.fori_loop(0, chunks, place, 0)
    for z in range(vertical):
        if z + 1 < vertical:
            tile = in_refs[z + 1][chunks * rows :, :]
        else:
            tile = tail_ref[...]
        for g in range(rows // SUBLANES):
            turned = tile if g == 0 else pltpu.roll(tile, LANES - g, 1)
            edge[pl.ds(z + g * SUBLANES * vertical, SUBLANES, stride=vertical), :] = turned
    for copy in copies:
        copy.wait()
    lane = lax.broadcasted_iota(jnp.int32, (vertical, LANES), 1)
    tall_lane = lax.broadcasted_iota(jnp.int32, (devices, LANES), 1)

    def padded(x):
        if devices == vertical:
            return x
        return jnp.concatenate([x, jnp.zeros((devices - vertical, LANES), jnp.float32)], axis=0)

    def one_cycle(r, carry):
        whole = lax.shift_right_logical(cells[r], LANE_BITS)
        part = cells[r] & (LANES - 1)
        turn_by = jnp.where(blocks[r] == 0, 0, devices - blocks[r])
        turn_more = devices - 1 - blocks[r]
        keep = jnp.full((vertical, LANES), 1.0 - fracs[r], jnp.float32)
        give = jnp.full((vertical, LANES), fracs[r], jnp.float32)
        inside = lane < part
        for f in range(fluids):
            row = f * cycles + r
            at = pl.ds(pl.multiple_of(row * vertical, vertical), vertical)
            near = [held[q, at, :] for q in range(chunks)]
            moved = [pltpu.roll(x, 1, 1) for x in near]
            turned = []
            for q in range(chunks):
                far = jnp.where(lane == 0, moved[q - 1] if q else edge[at, :], moved[q])
                turned.append(pltpu.roll(keep * near[q] + give * far, part, 1))
            to = pl.ds(pl.multiple_of(row * devices, devices), devices)
            for q in range(chunks):
                if q == 0:
                    value = jnp.where(
                        tall_lane < part,
                        pltpu.roll(padded(turned[chunks - 1]), turn_more, 0),
                        pltpu.roll(padded(turned[0]), turn_by, 0),
                    )
                else:
                    value = pltpu.roll(
                        padded(jnp.where(inside, turned[q - 1], turned[q])),
                        jnp.where(whole + q >= chunks, turn_more, turn_by),
                        0,
                    )
                sorted_ref[jnp.where(whole + q >= chunks, whole + q - chunks, whole + q), to, :] = value
        return carry

    lax.fori_loop(0, cycles, one_cycle, 0, unroll=8)
    def hand_out(q, carry):
        at = pl.ds(pl.multiple_of(q * LANES, LANES), LANES)
        for e in range(devices):
            out_refs[e][:, at] = sorted_ref[q, pl.ds(e, rows, stride=devices), :]
        return carry

    lax.fori_loop(0, chunks, hand_out, 0)


def vmem():
    return pl.BlockSpec(memory_space=pltpu.VMEM)


def turn(awaited, slices, tail, blocks, cells, fracs, fluids, width, devices):
    vertical = len(slices)
    cycles = cells.shape[0]
    rows = fluids * cycles
    out = jax.ShapeDtypeStruct((rows, width), jnp.float32)
    return pl.pallas_call(
        functools.partial(turn_kernel, vertical, devices, fluids, len(awaited)),
        out_shape=[out] * devices,
        in_specs=[pl.BlockSpec(memory_space=pl.ANY)] * (3 + len(awaited))
        + [vmem()] * (vertical + 1),
        scratch_shapes=[
            pltpu.SMEM((cycles,), jnp.int32),
            pltpu.SMEM((cycles,), jnp.int32),
            pltpu.SMEM((cycles,), jnp.float32),
            pltpu.VMEM((width // LANES, rows * vertical, LANES), jnp.float32),
            pltpu.VMEM((rows * vertical, LANES), jnp.float32),
            pltpu.VMEM((width // LANES, rows * devices, LANES), jnp.float32),
            pltpu.SemaphoreType.DMA((3,)),
        ],
        compiler_params=params(),
        cost_estimate=cost(0, 2 * rows * vertical * width * 4),
    )(blocks, cells, fracs, *awaited, *[slices[i] for i in first_order(vertical)], tail)


def coefficient_kernel(groups, own_ref, *refs):
    rank = lax.axis_index("rad")
    other_refs = refs[: groups - 1]
    coef_ref, table, inner, outer = refs[groups - 1 :]
    fluids, cycles = own_ref.shape
    total = groups * cycles

    for step in range(groups):
        source = partner_of(rank, step, groups)[1]
        ref = own_ref if step == 0 else other_refs[step - 1]

        def fill(r, carry, ref=ref, source=source):
            for f in range(fluids):
                table[f, source * cycles + r] = ref[f, r]
            return carry

        lax.fori_loop(0, cycles, fill, 0, unroll=8)

    def spans(f):
        return slice(f * LANES, (f + 1) * LANES)

    one = jnp.ones((1, LANES), jnp.float32)
    for f in range(fluids):
        inner[0, :, spans(f)] = one
        outer[total - 1, :, spans(f)] = one

    def march(s, carry):
        new = []
        for f in range(fluids):
            for way in range(2):
                low, high = carry[2 * f + way]
                link = jnp.full((1, LANES), table[f, s if way == 0 else total - s], jnp.float32)
                low = low + high / link
                if way == 0:
                    inner[s, :, spans(f)] = low
                else:
                    outer[total - 1 - s, :, spans(f)] = low
                new.append((low, high + low))
        return tuple(new)

    ends = lax.fori_loop(1, total, march, ((one, one),) * (2 * fluids))
    first = rank * cycles
    scales = [1.0 / ends[2 * f][1] for f in range(fluids)]

    def keep(r, carry):
        for f in range(fluids):
            coef_ref[0, r, :, spans(f)] = inner[first + r, :, spans(f)]
            coef_ref[1, r, :, spans(f)] = outer[first + r, :, spans(f)] * scales[f]
        return carry

    lax.fori_loop(0, cycles, keep, 0, unroll=8)


def coefficients(own, others):
    fluids, cycles = own.shape
    groups = len(others) + 1
    total = groups * cycles
    wide = fluids * LANES
    per_cycle = pltpu.VMEM((total, 1, wide), jnp.float32)
    return pl.pallas_call(
        functools.partial(coefficient_kernel, groups),
        out_shape=jax.ShapeDtypeStruct((2, cycles, 1, wide), jnp.float32),
        in_specs=[smem()] * groups,
        scratch_shapes=[pltpu.SMEM((fluids, total), jnp.float32), per_cycle, per_cycle],
        compiler_params=params(),
        cost_estimate=cost(0, 1 << 20),
    )(own, *others)


def coef_row(coef_ref, kind, r, f, chunks):
    row = coef_ref[kind, r, :, f * LANES : (f + 1) * LANES]
    return jnp.tile(row, (1, chunks))


def gather_kernel(vertical, devices, fluids, groups, block_table, cell_table, coef_ref, *refs):
    rank = lax.axis_index("rad")
    in_refs = restored(refs[:devices], second_order(devices))
    whole_ref = refs[devices]
    send_refs = refs[devices + 1 : devices + groups]
    blocks, cells, arrived, sems = refs[devices + groups :]
    copies = [
        pltpu.make_async_copy(block_table, blocks, sems.at[0]),
        pltpu.make_async_copy(cell_table, cells, sems.at[1]),
    ]
    for copy in copies:
        copy.start()
    chunks, rows = arrived.shape[0], arrived.shape[1] // devices
    width = chunks * LANES
    cycles = rows // fluids
    def place(q, carry):
        at = pl.ds(pl.multiple_of(q * LANES, LANES), LANES)
        for e in range(devices):
            arrived[q, pl.ds(e, rows, stride=devices), :] = in_refs[e][:, at]
        return carry

    lax.fori_loop(0, chunks, place, 0)
    for copy in copies:
        copy.wait()
    lane = lax.broadcasted_iota(jnp.int32, (vertical, width), 1)

    def one_cycle(r, carry):
        shift = cells[r]
        block = blocks[r]
        new = []
        for f in range(fluids):
            row = f * cycles + r
            at = pl.ds(pl.multiple_of(row * devices, devices), devices)
            held = jnp.concatenate([arrived[q, at, :] for q in range(chunks)], axis=1)
            first = pltpu.roll(held, block, 0)
            second = pltpu.roll(first, 1, 0)
            value = jnp.where(lane >= shift, first[:vertical], second[:vertical])
            whole_ref[pl.ds(pl.multiple_of(row * vertical, vertical), vertical), :] = value
            new.append(carry[2 * f] + coef_row(coef_ref, 0, r, f, chunks) * value)
            new.append(carry[2 * f + 1] + coef_row(coef_ref, 1, r, f, chunks) * value)
        return tuple(new)

    nothing = jnp.zeros((vertical, width), jnp.float32)
    sums = lax.fori_loop(0, cycles, one_cycle, (nothing,) * (2 * fluids), unroll=4)
    for step in range(1, groups):
        outward = partner_of(rank, step, groups)[0] > rank
        for f in range(fluids):
            send_refs[step - 1][f] = jnp.where(outward, sums[2 * f], sums[2 * f + 1])


def gather(pieces, blocks, cells, coef, fluids, vertical, groups):
    devices = len(pieces)
    rows, width = pieces[0].shape
    edge = jax.ShapeDtypeStruct((fluids, vertical, width), jnp.float32)
    return pl.pallas_call(
        functools.partial(gather_kernel, vertical, devices, fluids, groups),
        out_shape=[jax.ShapeDtypeStruct((rows * vertical, width), jnp.float32)]
        + [edge] * (groups - 1),
        in_specs=[pl.BlockSpec(memory_space=pl.ANY)] * 2 + [vmem()] * (devices + 1),
        scratch_shapes=[
            pltpu.SMEM(blocks.shape, jnp.int32),
            pltpu.SMEM(cells.shape, jnp.int32),
            pltpu.VMEM((width // LANES, rows * devices, LANES), jnp.float32),
            pltpu.SemaphoreType.DMA((2,)),
        ],
        compiler_params=params(),
        cost_estimate=cost(0, 2 * rows * vertical * width * 4),
    )(blocks, cells, coef, *[pieces[i] for i in second_order(devices)])


def scan_kernel(vertical, fluids, coef_ref, whole_ref, out_ref):
    width = whole_ref.shape[1]
    cycles = whole_ref.shape[0] // vertical // fluids
    chunks = width // LANES

    def at(f, r):
        return pl.ds(pl.multiple_of((f * cycles + r) * vertical, vertical), vertical)

    def upward(r, carry):
        new = []
        for f in range(fluids):
            total = carry[f] + coef_row(coef_ref, 0, r, f, chunks) * whole_ref[at(f, r), :]
            out_ref[at(f, r), :] = coef_row(coef_ref, 1, r, f, chunks) * total
            new.append(total)
        return tuple(new)

    def downward(s, carry):
        r = cycles - 1 - s
        new = []
        for f in range(fluids):
            out_ref[at(f, r), :] += coef_row(coef_ref, 0, r, f, chunks) * carry[f]
            new.append(carry[f] + coef_row(coef_ref, 1, r, f, chunks) * whole_ref[at(f, r), :])
        return tuple(new)

    nothing = jnp.zeros((vertical, width), jnp.float32)
    lax.fori_loop(0, cycles, upward, (nothing,) * fluids, unroll=4)
    lax.fori_loop(0, cycles, downward, (nothing,) * fluids, unroll=4)


def scans(coef, whole, vertical, fluids):
    return pl.pallas_call(
        functools.partial(scan_kernel, vertical, fluids),
        out_shape=jax.ShapeDtypeStruct(whole.shape, jnp.float32),
        compiler_params=params(),
        cost_estimate=cost(0, 3 * whole.size * 4),
    )(coef, whole)


def finish_kernel(vertical, fluids, groups, coef_ref, local_ref, *refs):
    rank = lax.axis_index("rad")
    in_refs = refs[: groups - 1][::-1]
    out_ref, done, sems = refs[groups - 1 :]
    width = local_ref.shape[1]
    cycles = local_ref.shape[0] // vertical // fluids
    chunks = width // LANES
    nothing = jnp.zeros((vertical, width), jnp.float32)
    entering = []
    for f in range(fluids):
        inward, outward = nothing, nothing
        for step in range(1, groups):
            value = in_refs[step - 1][f]
            from_inside = partner_of(rank, step, groups)[1] < rank
            inward = inward + jnp.where(from_inside, value, nothing)
            outward = outward + jnp.where(from_inside, nothing, value)
        entering += [inward, outward]

    parts = sems.shape[0]
    size = cycles // parts

    def copy_of(f, part):
        at = pl.ds((f * cycles + part * size) * vertical, size * vertical)
        return pltpu.make_async_copy(done.at[at], out_ref.at[at], sems.at[part, f])

    def one_cycle(r, carry):
        for f in range(fluids):
            at = pl.ds(pl.multiple_of((f * cycles + r) * vertical, vertical), vertical)
            done[at, :] = (
                local_ref[at, :]
                + coef_row(coef_ref, 1, r, f, chunks) * entering[2 * f]
                + coef_row(coef_ref, 0, r, f, chunks) * entering[2 * f + 1]
            )
        return carry

    for part in range(parts):
        lax.fori_loop(part * size, (part + 1) * size, one_cycle, 0, unroll=4)
        for f in range(fluids):
            copy_of(f, part).start()
    for part in range(parts):
        for f in range(fluids):
            copy_of(f, part).wait()


def finish(coef, local, arrived, vertical, fluids):
    groups = len(arrived) + 1
    return pl.pallas_call(
        functools.partial(finish_kernel, vertical, fluids, groups),
        out_shape=jax.ShapeDtypeStruct(local.shape, jnp.float32),
        in_specs=[vmem()] * (groups + 1),
        out_specs=hbm(),
        scratch_shapes=[
            pltpu.VMEM(local.shape, jnp.float32),
            pltpu.SemaphoreType.DMA((OUT_PARTS, fluids)),
        ],
        compiler_params=params(),
        cost_estimate=cost(0, 2 * local.size * 4),
    )(coef, local, *arrived[::-1])


def per_device(fields, cycle_blocks, cycle_cells, cycle_fracs, coupling):
    fluids, cycles, vertical, width = fields.shape
    devices = lax.axis_size("az")
    groups = lax.axis_size("rad")
    small = (coupling, cycle_blocks.reshape(cycles), cycle_cells, cycle_fracs)
    messages = spread(fields.reshape(fluids * cycles * vertical, width), small, vertical)
    slices = along_all(messages[:vertical], "az", range(vertical))
    tail, own, blocks, cells, fracs = messages[vertical:]
    if devices > vertical:
        tail = sent_along(tail, "az", vertical)
    far_first = sorted(range(1, groups), reverse=True)
    received = {step: exchanged(own, "rad", step) for step in far_first}
    others = [received[step] for step in range(1, groups)]

    pieces = turn(others, slices, tail, blocks, cells, fracs, fluids, width, devices)
    coef = coefficients(own, others)
    placed = along_all(pieces, "az", [(devices - e) % devices for e in range(devices)])
    whole, *ends_out = gather(placed, blocks, cells, coef, fluids, vertical, groups)
    received = {step: exchanged(ends_out[step - 1], "rad", step) for step in far_first}
    arrived = [received[step] for step in range(1, groups)]
    local = scans(coef, whole, vertical, fluids)
    solved = finish(coef, local, arrived, vertical, fluids)
    return solved.reshape(fields.shape)


def solution(mesh):
    return jax.shard_map(
        per_device,
        mesh=mesh,
        in_specs=(P(None, "rad", None, "az"), P("rad", None), P("rad"), P("rad"), P(None, "rad")),
        out_specs=P(None, "rad", None, "az"),
        check_vma=False,
    )
```

```python
import functools

import jax
import jax.numpy as jnp
from jax import lax
from jax.experimental import pallas as pl
from jax.experimental.pallas import tpu as pltpu
from jax.sharding import PartitionSpec as P

LANE_BITS = 7
LANES = 1 << LANE_BITS
SUBLANES = 8
VMEM_LIMIT = 24 * 1024 * 1024
OUT_PARTS = 4


def smem():
    return pl.BlockSpec(memory_space=pltpu.SMEM)


def params():
    return pltpu.CompilerParams(vmem_limit_bytes=VMEM_LIMIT)


def cost(flops, moved):
    return pl.CostEstimate(flops=flops, bytes_accessed=moved, transcendentals=0)


def sent_along(block, axis, distance):
    size = lax.axis_size(axis)
    return lax.ppermute(block, axis, [(i, (i + distance) % size) for i in range(size)])


def along_all(blocks, axis, distances):
    return [sent_along(b, axis, d) if d else b for b, d in zip(blocks, distances)]


def first_order(count):
    half = count // 2
    return sorted(range(count), key=lambda z: (z % 2, (1 - z % 2 * 2) * abs(z - half), -z))


def second_order(count):
    return sorted(range(count), key=lambda e: (count - e) % count)


def restored(refs, order):
    return [refs[order.index(i)] for i in range(len(order))]


def partner_of(rank, step, size):
    if size & (size - 1) == 0:
        return rank ^ step, rank ^ step
    return (rank + step) % size, (rank - step) % size


def exchanged(block, axis, step):
    size = lax.axis_size(axis)
    return lax.ppermute(block, axis, [(i, partner_of(i, step, size)[0]) for i in range(size)])


def hbm():
    return pl.BlockSpec(memory_space=pltpu.HBM)


def spread_kernel(vertical, small, x_ref, *refs):
    small_refs, refs = refs[:small], refs[small:]
    out_refs, refs = refs[: vertical + 1], refs[vertical + 1 :]
    passed_refs, (held, sems) = refs[:small], refs[small:]
    chunks, rows = held.shape[0], held.shape[1] // vertical
    copies = [
        pltpu.make_async_copy(x_ref.at[:, q * LANES : (q + 1) * LANES], held.at[q], sems.at[q])
        for q in reversed(range(chunks))
    ]
    passing = [
        pltpu.make_async_copy(small_refs[i], passed_refs[i], sems.at[chunks + i])
        for i in range(small)
    ]
    for copy in copies + passing:
        copy.start()
    lane = lax.broadcasted_iota(jnp.int32, (SUBLANES, LANES), 1)
    out_refs[0][chunks * rows :, :] = jnp.zeros((SUBLANES, LANES), jnp.float32)
    for q in reversed(range(chunks)):
        copies[chunks - 1 - q].wait()
        for z in range(vertical):
            part = held[q, pl.ds(z, rows, stride=vertical), :]
            out_refs[z][q * rows : (q + 1) * rows, :] = part
            if q == chunks - 1:
                tile = jnp.zeros((SUBLANES, LANES), jnp.float32)
                for g in range(rows // SUBLANES):
                    last = part[g * SUBLANES : (g + 1) * SUBLANES]
                    tile = jnp.where(lane == g, pltpu.roll(last, g + 1, 1), tile)
                if z + 1 < vertical:
                    out_refs[z + 1][chunks * rows :, :] = tile
                else:
                    out_refs[vertical][...] = tile
    for copy in passing:
        copy.wait()


def spread(x, passed, vertical):
    total, width = x.shape
    rows = total // vertical
    chunks = width // LANES
    main = jax.ShapeDtypeStruct((rows * chunks + SUBLANES, LANES), jnp.float32)
    tail = jax.ShapeDtypeStruct((SUBLANES, LANES), jnp.float32)
    return pl.pallas_call(
        functools.partial(spread_kernel, vertical, len(passed)),
        out_shape=[main] * vertical
        + [tail]
        + [jax.ShapeDtypeStruct(p.shape, p.dtype) for p in passed],
        in_specs=[hbm()] * (1 + len(passed)),
        scratch_shapes=[
            pltpu.VMEM((chunks, total, LANES), jnp.float32),
            pltpu.SemaphoreType.DMA((chunks + len(passed),)),
        ],
        compiler_params=params(),
        cost_estimate=cost(0, 2 * total * width * 4),
    )(*[pltpu.with_memory_space_constraint(a, pltpu.HBM) for a in (x, *passed)])


def turn_kernel(vertical, devices, fluids, awaited, *refs):
    tables, refs = refs[:3], refs[3 + awaited :]
    in_refs = restored(refs[:vertical], first_order(vertical))
    tail_ref = refs[vertical]
    out_refs = refs[vertical + 1 : vertical + 1 + devices]
    blocks, cells, fracs, held, edge, sorted_ref, sems = refs[vertical + 1 + devices :]
    chunks, rows = held.shape[0], held.shape[1] // vertical
    cycles = rows // fluids
    copies = [
        pltpu.make_async_copy(table, scalars, sems.at[i])
        for i, (table, scalars) in enumerate(zip(tables, (blocks, cells, fracs)))
    ]
    for copy in copies:
        copy.start()
    def place(q, carry):
        at = pl.ds(pl.multiple_of(q * rows, rows), rows)
        for z in range(vertical):
            held[q, pl.ds(z, rows, stride=vertical), :] = in_refs[z][at, :]
        return carry

    lax.fori_loop(0, chunks, place, 0)
    for z in range(vertical):
        if z + 1 < vertical:
            tile = in_refs[z + 1][chunks * rows :, :]
        else:
            tile = tail_ref[...]
        for g in range(rows // SUBLANES):
            edge[pl.ds(z + g * SUBLANES * vertical, SUBLANES, stride=vertical), :] = (
                jnp.broadcast_to(tile[:, g : g + 1], (SUBLANES, LANES))
            )
    for copy in copies:
        copy.wait()
    lane = lax.broadcasted_iota(jnp.int32, (vertical, LANES), 1)
    tall_lane = lax.broadcasted_iota(jnp.int32, (devices, LANES), 1)

    def padded(x):
        if devices == vertical:
            return x
        return jnp.concatenate([x, jnp.zeros((devices - vertical, LANES), jnp.float32)], axis=0)

    def one_cycle(r, carry):
        whole = lax.shift_right_logical(cells[r], LANE_BITS)
        part = cells[r] & (LANES - 1)
        turn_by = jnp.where(blocks[r] == 0, 0, devices - blocks[r])
        turn_more = devices - 1 - blocks[r]
        keep = jnp.full((vertical, LANES), 1.0 - fracs[r], jnp.float32)
        give = jnp.full((vertical, LANES), fracs[r], jnp.float32)
        inside = lane < part
        turns = [jnp.where(whole + q >= chunks, turn_more, turn_by) for q in range(chunks)]
        places = [lax.rem(whole + q, chunks) for q in range(chunks)]
        if chunks & (chunks - 1) == 0:
            places = [(whole + q) & (chunks - 1) for q in range(chunks)]
        for f in range(fluids):
            row = f * cycles + r
            at = pl.ds(pl.multiple_of(row * vertical, vertical), vertical)
            held_here = [held[q, at, :] for q in range(chunks)]
            at_cell = [pltpu.roll(x, part, 1) for x in held_here]
            before = [pltpu.roll(x, (part + 1) & (LANES - 1), 1) for x in held_here]
            to = pl.ds(pl.multiple_of(row * devices, devices), devices)
            for q in range(chunks):
                near = jnp.where(inside, at_cell[q - 1], at_cell[q])
                if q == 0:
                    far = jnp.where(lane == part, edge[at, :], before[0])
                    far = jnp.where(inside, before[chunks - 1], far)
                else:
                    far = jnp.where(lane <= part, before[q - 1], before[q])
                value = padded(keep * near + give * far)
                if q == 0:
                    value = jnp.where(
                        tall_lane < part,
                        pltpu.roll(value, turn_more, 0),
                        pltpu.roll(value, turn_by, 0),
                    )
                else:
                    value = pltpu.roll(value, turns[q], 0)
                sorted_ref[places[q], to, :] = value
        return carry

    lax.fori_loop(0, cycles, one_cycle, 0, unroll=8)
    def hand_out(q, carry):
        at = pl.ds(pl.multiple_of(q * LANES, LANES), LANES)
        for e in range(devices):
            out_refs[e][:, at] = sorted_ref[q, pl.ds(e, rows, stride=devices), :]
        return carry

    lax.fori_loop(0, chunks, hand_out, 0)


def vmem():
    return pl.BlockSpec(memory_space=pltpu.VMEM)


def turn(awaited, slices, tail, blocks, cells, fracs, fluids, width, devices):
    vertical = len(slices)
    cycles = cells.shape[0]
    rows = fluids * cycles
    out = jax.ShapeDtypeStruct((rows, width), jnp.float32)
    return pl.pallas_call(
        functools.partial(turn_kernel, vertical, devices, fluids, len(awaited)),
        out_shape=[out] * devices,
        in_specs=[pl.BlockSpec(memory_space=pl.ANY)] * (3 + len(awaited))
        + [vmem()] * (vertical + 1),
        scratch_shapes=[
            pltpu.SMEM((cycles,), jnp.int32),
            pltpu.SMEM((cycles,), jnp.int32),
            pltpu.SMEM((cycles,), jnp.float32),
            pltpu.VMEM((width // LANES, rows * vertical, LANES), jnp.float32),
            pltpu.VMEM((rows * vertical, LANES), jnp.float32),
            pltpu.VMEM((width // LANES, rows * devices, LANES), jnp.float32),
            pltpu.SemaphoreType.DMA((3,)),
        ],
        compiler_params=params(),
        cost_estimate=cost(0, 2 * rows * vertical * width * 4),
    )(blocks, cells, fracs, *awaited, *[slices[i] for i in first_order(vertical)], tail)


def coefficient_kernel(groups, own_ref, *refs):
    rank = lax.axis_index("rad")
    other_refs = refs[: groups - 1]
    coef_ref, table, inner, outer = refs[groups - 1 :]
    fluids, cycles = own_ref.shape
    total = groups * cycles

    for step in range(groups):
        source = partner_of(rank, step, groups)[1]
        ref = own_ref if step == 0 else other_refs[step - 1]

        def fill(r, carry, ref=ref, source=source):
            for f in range(fluids):
                table[f, source * cycles + r] = ref[f, r]
            return carry

        lax.fori_loop(0, cycles, fill, 0, unroll=8)

    def spans(f):
        return slice(f * LANES, (f + 1) * LANES)

    one = jnp.ones((1, LANES), jnp.float32)
    for f in range(fluids):
        inner[0, :, spans(f)] = one
        outer[total - 1, :, spans(f)] = one

    def march(s, carry):
        new = []
        for f in range(fluids):
            for way in range(2):
                low, high = carry[2 * f + way]
                link = jnp.full((1, LANES), table[f, s if way == 0 else total - s], jnp.float32)
                low = low + high / link
                if way == 0:
                    inner[s, :, spans(f)] = low
                else:
                    outer[total - 1 - s, :, spans(f)] = low
                new.append((low, high + low))
        return tuple(new)

    ends = lax.fori_loop(1, total, march, ((one, one),) * (2 * fluids))
    first = rank * cycles
    scales = [1.0 / ends[2 * f][1] for f in range(fluids)]

    def keep(r, carry):
        for f in range(fluids):
            coef_ref[0, r, :, spans(f)] = inner[first + r, :, spans(f)]
            coef_ref[1, r, :, spans(f)] = outer[first + r, :, spans(f)] * scales[f]
        return carry

    lax.fori_loop(0, cycles, keep, 0, unroll=8)


def coefficients(own, others):
    fluids, cycles = own.shape
    groups = len(others) + 1
    total = groups * cycles
    wide = fluids * LANES
    per_cycle = pltpu.VMEM((total, 1, wide), jnp.float32)
    return pl.pallas_call(
        functools.partial(coefficient_kernel, groups),
        out_shape=jax.ShapeDtypeStruct((2, cycles, 1, wide), jnp.float32),
        in_specs=[smem()] * groups,
        scratch_shapes=[pltpu.SMEM((fluids, total), jnp.float32), per_cycle, per_cycle],
        compiler_params=params(),
        cost_estimate=cost(0, 1 << 20),
    )(own, *others)


def coef_row(coef_ref, kind, r, f, chunks):
    row = coef_ref[kind, r, :, f * LANES : (f + 1) * LANES]
    return jnp.tile(row, (1, chunks))


def gather_kernel(vertical, devices, fluids, groups, block_table, cell_table, coef_ref, *refs):
    rank = lax.axis_index("rad")
    in_refs = restored(refs[:devices], second_order(devices))
    whole_ref = refs[devices]
    send_refs = refs[devices + 1 : devices + groups]
    blocks, cells, arrived, sems = refs[devices + groups :]
    copies = [
        pltpu.make_async_copy(block_table, blocks, sems.at[0]),
        pltpu.make_async_copy(cell_table, cells, sems.at[1]),
    ]
    for copy in copies:
        copy.start()
    chunks, rows = arrived.shape[0], arrived.shape[1] // devices
    width = chunks * LANES
    cycles = rows // fluids
    def place(q, carry):
        at = pl.ds(pl.multiple_of(q * LANES, LANES), LANES)
        for e in range(devices):
            arrived[q, pl.ds(e, rows, stride=devices), :] = in_refs[e][:, at]
        return carry

    lax.fori_loop(0, chunks, place, 0)
    for copy in copies:
        copy.wait()
    lane = lax.broadcasted_iota(jnp.int32, (vertical, width), 1)

    def one_cycle(r, carry):
        shift = cells[r]
        block = blocks[r]
        new = []
        for f in range(fluids):
            row = f * cycles + r
            at = pl.ds(pl.multiple_of(row * devices, devices), devices)
            held = jnp.concatenate([arrived[q, at, :] for q in range(chunks)], axis=1)
            first = pltpu.roll(held, block, 0)
            second = pltpu.roll(first, 1, 0)
            value = jnp.where(lane >= shift, first[:vertical], second[:vertical])
            whole_ref[pl.ds(pl.multiple_of(row * vertical, vertical), vertical), :] = value
            new.append(carry[2 * f] + coef_row(coef_ref, 0, r, f, chunks) * value)
            new.append(carry[2 * f + 1] + coef_row(coef_ref, 1, r, f, chunks) * value)
        return tuple(new)

    nothing = jnp.zeros((vertical, width), jnp.float32)
    sums = lax.fori_loop(0, cycles, one_cycle, (nothing,) * (2 * fluids), unroll=4)
    for step in range(1, groups):
        outward = partner_of(rank, step, groups)[0] > rank
        for f in range(fluids):
            send_refs[step - 1][f] = jnp.where(outward, sums[2 * f], sums[2 * f + 1])


def gather(pieces, blocks, cells, coef, fluids, vertical, groups):
    devices = len(pieces)
    rows, width = pieces[0].shape
    edge = jax.ShapeDtypeStruct((fluids, vertical, width), jnp.float32)
    return pl.pallas_call(
        functools.partial(gather_kernel, vertical, devices, fluids, groups),
        out_shape=[jax.ShapeDtypeStruct((rows * vertical, width), jnp.float32)]
        + [edge] * (groups - 1),
        in_specs=[pl.BlockSpec(memory_space=pl.ANY)] * 2 + [vmem()] * (devices + 1),
        scratch_shapes=[
            pltpu.SMEM(blocks.shape, jnp.int32),
            pltpu.SMEM(cells.shape, jnp.int32),
            pltpu.VMEM((width // LANES, rows * devices, LANES), jnp.float32),
            pltpu.SemaphoreType.DMA((2,)),
        ],
        compiler_params=params(),
        cost_estimate=cost(0, 2 * rows * vertical * width * 4),
    )(blocks, cells, coef, *[pieces[i] for i in second_order(devices)])


def scan_kernel(vertical, fluids, coef_ref, whole_ref, out_ref):
    width = whole_ref.shape[1]
    cycles = whole_ref.shape[0] // vertical // fluids
    chunks = width // LANES

    def at(f, r):
        return pl.ds(pl.multiple_of((f * cycles + r) * vertical, vertical), vertical)

    def upward(r, carry):
        new = []
        for f in range(fluids):
            total = carry[f] + coef_row(coef_ref, 0, r, f, chunks) * whole_ref[at(f, r), :]
            out_ref[at(f, r), :] = coef_row(coef_ref, 1, r, f, chunks) * total
            new.append(total)
        return tuple(new)

    def downward(s, carry):
        r = cycles - 1 - s
        new = []
        for f in range(fluids):
            out_ref[at(f, r), :] += coef_row(coef_ref, 0, r, f, chunks) * carry[f]
            new.append(carry[f] + coef_row(coef_ref, 1, r, f, chunks) * whole_ref[at(f, r), :])
        return tuple(new)

    nothing = jnp.zeros((vertical, width), jnp.float32)
    lax.fori_loop(0, cycles, upward, (nothing,) * fluids, unroll=4)
    lax.fori_loop(0, cycles, downward, (nothing,) * fluids, unroll=4)


def scans(coef, whole, vertical, fluids):
    return pl.pallas_call(
        functools.partial(scan_kernel, vertical, fluids),
        out_shape=jax.ShapeDtypeStruct(whole.shape, jnp.float32),
        compiler_params=params(),
        cost_estimate=cost(0, 3 * whole.size * 4),
    )(coef, whole)


def finish_kernel(vertical, fluids, groups, coef_ref, local_ref, *refs):
    rank = lax.axis_index("rad")
    in_refs = refs[: groups - 1][::-1]
    out_ref, done, sems = refs[groups - 1 :]
    width = local_ref.shape[1]
    cycles = local_ref.shape[0] // vertical // fluids
    chunks = width // LANES
    nothing = jnp.zeros((vertical, width), jnp.float32)
    entering = []
    for f in range(fluids):
        inward, outward = nothing, nothing
        for step in range(1, groups):
            value = in_refs[step - 1][f]
            from_inside = partner_of(rank, step, groups)[1] < rank
            inward = inward + jnp.where(from_inside, value, nothing)
            outward = outward + jnp.where(from_inside, nothing, value)
        entering += [inward, outward]

    parts = sems.shape[0]
    size = cycles // parts

    def copy_of(f, part):
        at = pl.ds((f * cycles + part * size) * vertical, size * vertical)
        return pltpu.make_async_copy(done.at[at], out_ref.at[at], sems.at[part, f])

    def one_cycle(r, carry):
        for f in range(fluids):
            at = pl.ds(pl.multiple_of((f * cycles + r) * vertical, vertical), vertical)
            done[at, :] = (
                local_ref[at, :]
                + coef_row(coef_ref, 1, r, f, chunks) * entering[2 * f]
                + coef_row(coef_ref, 0, r, f, chunks) * entering[2 * f + 1]
            )
        return carry

    for part in range(parts):
        lax.fori_loop(part * size, (part + 1) * size, one_cycle, 0, unroll=4)
        for f in range(fluids):
            copy_of(f, part).start()
    for part in range(parts):
        for f in range(fluids):
            copy_of(f, part).wait()


def finish(coef, local, arrived, vertical, fluids):
    groups = len(arrived) + 1
    return pl.pallas_call(
        functools.partial(finish_kernel, vertical, fluids, groups),
        out_shape=jax.ShapeDtypeStruct(local.shape, jnp.float32),
        in_specs=[vmem()] * (groups + 1),
        out_specs=hbm(),
        scratch_shapes=[
            pltpu.VMEM(local.shape, jnp.float32),
            pltpu.SemaphoreType.DMA((OUT_PARTS, fluids)),
        ],
        compiler_params=params(),
        cost_estimate=cost(0, 2 * local.size * 4),
    )(coef, local, *arrived[::-1])


def per_device(fields, cycle_blocks, cycle_cells, cycle_fracs, coupling):
    fluids, cycles, vertical, width = fields.shape
    devices = lax.axis_size("az")
    groups = lax.axis_size("rad")
    small = (coupling, cycle_blocks.reshape(cycles), cycle_cells, cycle_fracs)
    messages = spread(fields.reshape(fluids * cycles * vertical, width), small, vertical)
    slices = along_all(messages[:vertical], "az", range(vertical))
    tail, own, blocks, cells, fracs = messages[vertical:]
    if devices > vertical:
        tail = sent_along(tail, "az", vertical)
    far_first = sorted(range(1, groups), reverse=True)
    received = {step: exchanged(own, "rad", step) for step in far_first}
    others = [received[step] for step in range(1, groups)]

    pieces = turn(others, slices, tail, blocks, cells, fracs, fluids, width, devices)
    coef = coefficients(own, others)
    placed = along_all(pieces, "az", [(devices - e) % devices for e in range(devices)])
    whole, *ends_out = gather(placed, blocks, cells, coef, fluids, vertical, groups)
    received = {step: exchanged(ends_out[step - 1], "rad", step) for step in far_first}
    arrived = [received[step] for step in range(1, groups)]
    local = scans(coef, whole, vertical, fluids)
    solved = finish(coef, local, arrived, vertical, fluids)
    return solved.reshape(fields.shape)


def solution(mesh):
    return jax.shard_map(
        per_device,
        mesh=mesh,
        in_specs=(P(None, "rad", None, "az"), P("rad", None), P("rad"), P("rad"), P(None, "rad")),
        out_specs=P(None, "rad", None, "az"),
        check_vma=False,
    )
```

```python
import functools

import jax
import jax.numpy as jnp
from jax import lax
from jax.experimental import pallas as pl
from jax.experimental.pallas import tpu as pltpu
from jax.sharding import PartitionSpec as P

LANE_BITS = 7
LANES = 1 << LANE_BITS
SUBLANES = 8
VMEM_LIMIT = 24 * 1024 * 1024
OUT_PARTS = 4


def smem():
    return pl.BlockSpec(memory_space=pltpu.SMEM)


def params():
    return pltpu.CompilerParams(vmem_limit_bytes=VMEM_LIMIT)


def cost(flops, moved):
    return pl.CostEstimate(flops=flops, bytes_accessed=moved, transcendentals=0)


def sent_along(block, axis, distance):
    size = lax.axis_size(axis)
    return lax.ppermute(block, axis, [(i, (i + distance) % size) for i in range(size)])


def along_all(blocks, axis, distances):
    return [sent_along(b, axis, d) if d else b for b, d in zip(blocks, distances)]


def first_order(count):
    half = count // 2
    return sorted(range(count), key=lambda z: (z % 2, (1 - z % 2 * 2) * abs(z - half), -z))


def second_order(count):
    distance = [(count - e) % count for e in range(count)]
    return sorted(range(count), key=lambda e: 3.5 if distance[e] == 2 else distance[e])


def restored(refs, order):
    return [refs[order.index(i)] for i in range(len(order))]


def partner_of(rank, step, size):
    if size & (size - 1) == 0:
        return rank ^ step, rank ^ step
    return (rank + step) % size, (rank - step) % size


def exchanged(block, axis, step):
    size = lax.axis_size(axis)
    return lax.ppermute(block, axis, [(i, partner_of(i, step, size)[0]) for i in range(size)])


def hbm():
    return pl.BlockSpec(memory_space=pltpu.HBM)


def spread_kernel(vertical, small, x_ref, *refs):
    small_refs, refs = refs[:small], refs[small:]
    out_refs, refs = refs[: vertical + 1], refs[vertical + 1 :]
    passed_refs, (held, sems) = refs[:small], refs[small:]
    chunks, rows = held.shape[0], held.shape[1] // vertical
    copies = [
        pltpu.make_async_copy(x_ref.at[:, q * LANES : (q + 1) * LANES], held.at[q], sems.at[q])
        for q in reversed(range(chunks))
    ]
    passing = [
        pltpu.make_async_copy(small_refs[i], passed_refs[i], sems.at[chunks + i])
        for i in range(small)
    ]
    for copy in copies + passing:
        copy.start()
    lane = lax.broadcasted_iota(jnp.int32, (SUBLANES, LANES), 1)
    out_refs[0][chunks * rows :, :] = jnp.zeros((SUBLANES, LANES), jnp.float32)
    for q in reversed(range(chunks)):
        copies[chunks - 1 - q].wait()
        for z in range(vertical):
            part = held[q, pl.ds(z, rows, stride=vertical), :]
            out_refs[z][q * rows : (q + 1) * rows, :] = part
            if q == chunks - 1:
                tile = jnp.zeros((SUBLANES, LANES), jnp.float32)
                for g in range(rows // SUBLANES):
                    last = part[g * SUBLANES : (g + 1) * SUBLANES]
                    tile = jnp.where(lane == g, pltpu.roll(last, g + 1, 1), tile)
                if z + 1 < vertical:
                    out_refs[z + 1][chunks * rows :, :] = tile
                else:
                    out_refs[vertical][...] = tile
    for copy in passing:
        copy.wait()


def spread(x, passed, vertical):
    total, width = x.shape
    rows = total // vertical
    chunks = width // LANES
    main = jax.ShapeDtypeStruct((rows * chunks + SUBLANES, LANES), jnp.float32)
    tail = jax.ShapeDtypeStruct((SUBLANES, LANES), jnp.float32)
    return pl.pallas_call(
        functools.partial(spread_kernel, vertical, len(passed)),
        out_shape=[main] * vertical
        + [tail]
        + [jax.ShapeDtypeStruct(p.shape, p.dtype) for p in passed],
        in_specs=[hbm()] * (1 + len(passed)),
        scratch_shapes=[
            pltpu.VMEM((chunks, total, LANES), jnp.float32),
            pltpu.SemaphoreType.DMA((chunks + len(passed),)),
        ],
        compiler_params=params(),
        cost_estimate=cost(0, 2 * total * width * 4),
    )(*[pltpu.with_memory_space_constraint(a, pltpu.HBM) for a in (x, *passed)])


def turn_kernel(vertical, devices, fluids, awaited, *refs):
    tables, refs = refs[:3], refs[3 + awaited :]
    in_refs = restored(refs[:vertical], first_order(vertical))
    tail_ref = refs[vertical]
    out_refs = refs[vertical + 1 : vertical + 1 + devices]
    blocks, cells, fracs, held, edge, sorted_ref, sems = refs[vertical + 1 + devices :]
    chunks, rows = held.shape[0], held.shape[1] // vertical
    cycles = rows // fluids
    copies = [
        pltpu.make_async_copy(table, scalars, sems.at[i])
        for i, (table, scalars) in enumerate(zip(tables, (blocks, cells, fracs)))
    ]
    for copy in copies:
        copy.start()
    def place(q, carry):
        at = pl.ds(pl.multiple_of(q * rows, rows), rows)
        for z in range(vertical):
            held[q, pl.ds(z, rows, stride=vertical), :] = in_refs[z][at, :]
        return carry

    lax.fori_loop(0, chunks, place, 0)
    for z in range(vertical):
        if z + 1 < vertical:
            tile = in_refs[z + 1][chunks * rows :, :]
        else:
            tile = tail_ref[...]
        for g in range(rows // SUBLANES):
            edge[pl.ds(z + g * SUBLANES * vertical, SUBLANES, stride=vertical), :] = (
                jnp.broadcast_to(tile[:, g : g + 1], (SUBLANES, LANES))
            )
    for copy in copies:
        copy.wait()
    lane = lax.broadcasted_iota(jnp.int32, (vertical, LANES), 1)
    tall_lane = lax.broadcasted_iota(jnp.int32, (devices, LANES), 1)

    def padded(x):
        if devices == vertical:
            return x
        return jnp.concatenate([x, jnp.zeros((devices - vertical, LANES), jnp.float32)], axis=0)

    def one_cycle(r, carry):
        whole = lax.shift_right_logical(cells[r], LANE_BITS)
        part = cells[r] & (LANES - 1)
        turn_by = jnp.where(blocks[r] == 0, 0, devices - blocks[r])
        turn_more = devices - 1 - blocks[r]
        keep = jnp.full((vertical, LANES), 1.0 - fracs[r], jnp.float32)
        give = jnp.full((vertical, LANES), fracs[r], jnp.float32)
        inside = lane < part
        turns = [jnp.where(whole + q >= chunks, turn_more, turn_by) for q in range(chunks)]
        places = [lax.rem(whole + q, chunks) for q in range(chunks)]
        if chunks & (chunks - 1) == 0:
            places = [(whole + q) & (chunks - 1) for q in range(chunks)]
        for f in range(fluids):
            row = f * cycles + r
            at = pl.ds(pl.multiple_of(row * vertical, vertical), vertical)
            held_here = [held[q, at, :] for q in range(chunks)]
            at_cell = [pltpu.roll(x, part, 1) for x in held_here]
            before = [pltpu.roll(x, (part + 1) & (LANES - 1), 1) for x in held_here]
            to = pl.ds(pl.multiple_of(row * devices, devices), devices)
            for q in range(chunks):
                near = jnp.where(inside, at_cell[q - 1], at_cell[q])
                if q == 0:
                    far = jnp.where(lane == part, edge[at, :], before[0])
                    far = jnp.where(inside, before[chunks - 1], far)
                else:
                    far = jnp.where(lane <= part, before[q - 1], before[q])
                value = padded(keep * near + give * far)
                if q == 0:
                    value = jnp.where(
                        tall_lane < part,
                        pltpu.roll(value, turn_more, 0),
                        pltpu.roll(value, turn_by, 0),
                    )
                else:
                    value = pltpu.roll(value, turns[q], 0)
                sorted_ref[places[q], to, :] = value
        return carry

    lax.fori_loop(0, cycles, one_cycle, 0, unroll=8)
    def hand_out(q, carry):
        at = pl.ds(pl.multiple_of(q * LANES, LANES), LANES)
        for e in range(devices):
            out_refs[e][:, at] = sorted_ref[q, pl.ds(e, rows, stride=devices), :]
        return carry

    lax.fori_loop(0, chunks, hand_out, 0)


def vmem():
    return pl.BlockSpec(memory_space=pltpu.VMEM)


def turn(awaited, slices, tail, blocks, cells, fracs, fluids, width, devices):
    vertical = len(slices)
    cycles = cells.shape[0]
    rows = fluids * cycles
    out = jax.ShapeDtypeStruct((rows, width), jnp.float32)
    return pl.pallas_call(
        functools.partial(turn_kernel, vertical, devices, fluids, len(awaited)),
        out_shape=[out] * devices,
        in_specs=[pl.BlockSpec(memory_space=pl.ANY)] * (3 + len(awaited))
        + [vmem()] * (vertical + 1),
        scratch_shapes=[
            pltpu.SMEM((cycles,), jnp.int32),
            pltpu.SMEM((cycles,), jnp.int32),
            pltpu.SMEM((cycles,), jnp.float32),
            pltpu.VMEM((width // LANES, rows * vertical, LANES), jnp.float32),
            pltpu.VMEM((rows * vertical, LANES), jnp.float32),
            pltpu.VMEM((width // LANES, rows * devices, LANES), jnp.float32),
            pltpu.SemaphoreType.DMA((3,)),
        ],
        compiler_params=params(),
        cost_estimate=cost(0, 2 * rows * vertical * width * 4),
    )(blocks, cells, fracs, *awaited, *[slices[i] for i in first_order(vertical)], tail)


def coefficient_kernel(groups, own_ref, *refs):
    rank = lax.axis_index("rad")
    other_refs = refs[: groups - 1]
    coef_ref, table, inner, outer = refs[groups - 1 :]
    fluids, cycles = own_ref.shape
    total = groups * cycles

    for step in range(groups):
        source = partner_of(rank, step, groups)[1]
        ref = own_ref if step == 0 else other_refs[step - 1]

        def fill(r, carry, ref=ref, source=source):
            for f in range(fluids):
                table[f, source * cycles + r] = ref[f, r]
            return carry

        lax.fori_loop(0, cycles, fill, 0, unroll=8)

    def spans(f):
        return slice(f * LANES, (f + 1) * LANES)

    one = jnp.ones((1, LANES), jnp.float32)
    for f in range(fluids):
        inner[0, :, spans(f)] = one
        outer[total - 1, :, spans(f)] = one

    def march(s, carry):
        new = []
        for f in range(fluids):
            for way in range(2):
                low, high = carry[2 * f + way]
                link = jnp.full((1, LANES), table[f, s if way == 0 else total - s], jnp.float32)
                low = low + high / link
                if way == 0:
                    inner[s, :, spans(f)] = low
                else:
                    outer[total - 1 - s, :, spans(f)] = low
                new.append((low, high + low))
        return tuple(new)

    ends = lax.fori_loop(1, total, march, ((one, one),) * (2 * fluids))
    first = rank * cycles
    scales = [1.0 / ends[2 * f][1] for f in range(fluids)]

    def keep(r, carry):
        for f in range(fluids):
            coef_ref[0, r, :, spans(f)] = inner[first + r, :, spans(f)]
            coef_ref[1, r, :, spans(f)] = outer[first + r, :, spans(f)] * scales[f]
        return carry

    lax.fori_loop(0, cycles, keep, 0, unroll=8)


def coefficients(own, others):
    fluids, cycles = own.shape
    groups = len(others) + 1
    total = groups * cycles
    wide = fluids * LANES
    per_cycle = pltpu.VMEM((total, 1, wide), jnp.float32)
    return pl.pallas_call(
        functools.partial(coefficient_kernel, groups),
        out_shape=jax.ShapeDtypeStruct((2, cycles, 1, wide), jnp.float32),
        in_specs=[smem()] * groups,
        scratch_shapes=[pltpu.SMEM((fluids, total), jnp.float32), per_cycle, per_cycle],
        compiler_params=params(),
        cost_estimate=cost(0, 1 << 20),
    )(own, *others)


def coef_row(coef_ref, kind, r, f, chunks):
    row = coef_ref[kind, r, :, f * LANES : (f + 1) * LANES]
    return jnp.tile(row, (1, chunks))


def gather_kernel(vertical, devices, fluids, groups, block_table, cell_table, coef_ref, *refs):
    rank = lax.axis_index("rad")
    in_refs = restored(refs[:devices], second_order(devices))
    whole_ref = refs[devices]
    send_refs = refs[devices + 1 : devices + groups]
    blocks, cells, arrived, sems = refs[devices + groups :]
    copies = [
        pltpu.make_async_copy(block_table, blocks, sems.at[0]),
        pltpu.make_async_copy(cell_table, cells, sems.at[1]),
    ]
    for copy in copies:
        copy.start()
    chunks, rows = arrived.shape[0], arrived.shape[1] // devices
    width = chunks * LANES
    cycles = rows // fluids
    def place(q, carry):
        at = pl.ds(pl.multiple_of(q * LANES, LANES), LANES)
        for e in range(devices):
            arrived[q, pl.ds(e, rows, stride=devices), :] = in_refs[e][:, at]
        return carry

    lax.fori_loop(0, chunks, place, 0)
    for copy in copies:
        copy.wait()
    lane = lax.broadcasted_iota(jnp.int32, (vertical, width), 1)

    def one_cycle(r, carry):
        shift = cells[r]
        block = blocks[r]
        new = []
        for f in range(fluids):
            row = f * cycles + r
            at = pl.ds(pl.multiple_of(row * devices, devices), devices)
            held = jnp.concatenate([arrived[q, at, :] for q in range(chunks)], axis=1)
            first = pltpu.roll(held, block, 0)
            second = pltpu.roll(first, 1, 0)
            value = jnp.where(lane >= shift, first[:vertical], second[:vertical])
            whole_ref[pl.ds(pl.multiple_of(row * vertical, vertical), vertical), :] = value
            new.append(carry[2 * f] + coef_row(coef_ref, 0, r, f, chunks) * value)
            new.append(carry[2 * f + 1] + coef_row(coef_ref, 1, r, f, chunks) * value)
        return tuple(new)

    nothing = jnp.zeros((vertical, width), jnp.float32)
    sums = lax.fori_loop(0, cycles, one_cycle, (nothing,) * (2 * fluids), unroll=4)
    for step in range(1, groups):
        outward = partner_of(rank, step, groups)[0] > rank
        for f in range(fluids):
            send_refs[step - 1][f] = jnp.where(outward, sums[2 * f], sums[2 * f + 1])


def gather(pieces, blocks, cells, coef, fluids, vertical, groups):
    devices = len(pieces)
    rows, width = pieces[0].shape
    edge = jax.ShapeDtypeStruct((fluids, vertical, width), jnp.float32)
    return pl.pallas_call(
        functools.partial(gather_kernel, vertical, devices, fluids, groups),
        out_shape=[jax.ShapeDtypeStruct((rows * vertical, width), jnp.float32)]
        + [edge] * (groups - 1),
        in_specs=[pl.BlockSpec(memory_space=pl.ANY)] * 2 + [vmem()] * (devices + 1),
        scratch_shapes=[
            pltpu.SMEM(blocks.shape, jnp.int32),
            pltpu.SMEM(cells.shape, jnp.int32),
            pltpu.VMEM((width // LANES, rows * devices, LANES), jnp.float32),
            pltpu.SemaphoreType.DMA((2,)),
        ],
        compiler_params=params(),
        cost_estimate=cost(0, 2 * rows * vertical * width * 4),
    )(blocks, cells, coef, *[pieces[i] for i in second_order(devices)])


def scan_kernel(vertical, fluids, coef_ref, whole_ref, out_ref):
    width = whole_ref.shape[1]
    cycles = whole_ref.shape[0] // vertical // fluids
    chunks = width // LANES

    def at(f, r):
        return pl.ds(pl.multiple_of((f * cycles + r) * vertical, vertical), vertical)

    def upward(r, carry):
        new = []
        for f in range(fluids):
            total = carry[f] + coef_row(coef_ref, 0, r, f, chunks) * whole_ref[at(f, r), :]
            out_ref[at(f, r), :] = coef_row(coef_ref, 1, r, f, chunks) * total
            new.append(total)
        return tuple(new)

    def downward(s, carry):
        r = cycles - 1 - s
        new = []
        for f in range(fluids):
            out_ref[at(f, r), :] += coef_row(coef_ref, 0, r, f, chunks) * carry[f]
            new.append(carry[f] + coef_row(coef_ref, 1, r, f, chunks) * whole_ref[at(f, r), :])
        return tuple(new)

    nothing = jnp.zeros((vertical, width), jnp.float32)
    lax.fori_loop(0, cycles, upward, (nothing,) * fluids, unroll=4)
    lax.fori_loop(0, cycles, downward, (nothing,) * fluids, unroll=4)


def scans(coef, whole, vertical, fluids):
    return pl.pallas_call(
        functools.partial(scan_kernel, vertical, fluids),
        out_shape=jax.ShapeDtypeStruct(whole.shape, jnp.float32),
        compiler_params=params(),
        cost_estimate=cost(0, 3 * whole.size * 4),
    )(coef, whole)


def finish_kernel(vertical, fluids, groups, coef_ref, local_ref, *refs):
    rank = lax.axis_index("rad")
    in_refs = refs[: groups - 1][::-1]
    out_ref, done, sems = refs[groups - 1 :]
    width = local_ref.shape[1]
    cycles = local_ref.shape[0] // vertical // fluids
    chunks = width // LANES
    nothing = jnp.zeros((vertical, width), jnp.float32)
    entering = []
    for f in range(fluids):
        inward, outward = nothing, nothing
        for step in range(1, groups):
            value = in_refs[step - 1][f]
            from_inside = partner_of(rank, step, groups)[1] < rank
            inward = inward + jnp.where(from_inside, value, nothing)
            outward = outward + jnp.where(from_inside, nothing, value)
        entering += [inward, outward]

    parts = sems.shape[0]
    size = cycles // parts

    def copy_of(f, part):
        at = pl.ds((f * cycles + part * size) * vertical, size * vertical)
        return pltpu.make_async_copy(done.at[at], out_ref.at[at], sems.at[part, f])

    def one_cycle(r, carry):
        for f in range(fluids):
            at = pl.ds(pl.multiple_of((f * cycles + r) * vertical, vertical), vertical)
            done[at, :] = (
                local_ref[at, :]
                + coef_row(coef_ref, 1, r, f, chunks) * entering[2 * f]
                + coef_row(coef_ref, 0, r, f, chunks) * entering[2 * f + 1]
            )
        return carry

    for part in range(parts):
        lax.fori_loop(part * size, (part + 1) * size, one_cycle, 0, unroll=4)
        for f in range(fluids):
            copy_of(f, part).start()
    for part in range(parts):
        for f in range(fluids):
            copy_of(f, part).wait()


def finish(coef, local, arrived, vertical, fluids):
    groups = len(arrived) + 1
    return pl.pallas_call(
        functools.partial(finish_kernel, vertical, fluids, groups),
        out_shape=jax.ShapeDtypeStruct(local.shape, jnp.float32),
        in_specs=[vmem()] * (groups + 1),
        out_specs=hbm(),
        scratch_shapes=[
            pltpu.VMEM(local.shape, jnp.float32),
            pltpu.SemaphoreType.DMA((OUT_PARTS, fluids)),
        ],
        compiler_params=params(),
        cost_estimate=cost(0, 2 * local.size * 4),
    )(coef, local, *arrived[::-1])


def per_device(fields, cycle_blocks, cycle_cells, cycle_fracs, coupling):
    fluids, cycles, vertical, width = fields.shape
    devices = lax.axis_size("az")
    groups = lax.axis_size("rad")
    small = (coupling, cycle_blocks.reshape(cycles), cycle_cells, cycle_fracs)
    messages = spread(fields.reshape(fluids * cycles * vertical, width), small, vertical)
    slices = along_all(messages[:vertical], "az", range(vertical))
    tail, own, blocks, cells, fracs = messages[vertical:]
    if devices > vertical:
        tail = sent_along(tail, "az", vertical)
    far_first = sorted(range(1, groups), reverse=True)
    received = {step: exchanged(own, "rad", step) for step in far_first}
    others = [received[step] for step in range(1, groups)]

    pieces = turn(others, slices, tail, blocks, cells, fracs, fluids, width, devices)
    coef = coefficients(own, others)
    placed = along_all(pieces, "az", [(devices - e) % devices for e in range(devices)])
    whole, *ends_out = gather(placed, blocks, cells, coef, fluids, vertical, groups)
    received = {step: exchanged(ends_out[step - 1], "rad", step) for step in far_first}
    arrived = [received[step] for step in range(1, groups)]
    local = scans(coef, whole, vertical, fluids)
    solved = finish(coef, local, arrived, vertical, fluids)
    return solved.reshape(fields.shape)


def solution(mesh):
    return jax.shard_map(
        per_device,
        mesh=mesh,
        in_specs=(P(None, "rad", None, "az"), P("rad", None), P("rad"), P("rad"), P(None, "rad")),
        out_specs=P(None, "rad", None, "az"),
        check_vma=False,
    )
```
